256 devices in a mesh: tile: 64 (over z, y, x_lo), rot: 4 (over x_hi, core).
Axes of the slice: x: 4 (x_hi: 2, x_lo: 2; x = x_hi * 2 + x_lo), y: 4, z: 8, core: 2. Of those that a mesh axis runs over, the one named last changes fastest.
Arguments:
- tomogram: bfloat16 [1024, 128, 128], P('tile'), may hold values from -6 to 6
- templates: bfloat16 [64, 32, 32, 32], P('tile'), may hold values from -6 to 6
- owners: int32 [1], replicated, may hold values from 0 to 63
- orient_ids: int32 [1, 4], P(None, 'rot'), may hold values from 0 to 23
- slice_mask: int32 [1024], P('tile'), may hold values 0 or 1
Outputs:
- best_score: float32 [1024, 128, 128], P('tile')
The draws below stay inside these ranges and needn't reach their ends.
All inputs are finite; a program needn't handle non-finite values. No bound on the sum of `slice_mask` on one device may be relied on, other than what follows from the above.
Results may differ from the reference program's by a relative error of at most 0.012.
Values may be sent and summed in bfloat16 or wider, within the bound.
No kernel may reach another device: no remote copies, remote signals or barrier semaphores. Data moves between devices by JAX's collectives and lax.ppermute only.
A program may use at most 64 MiB of HBM per device.

```python
import math
import jax
import jax.numpy as jnp
from jax import lax

TS = 32
LY = 128
LZ = 128
CX = 16
STEPS = 1
ORIENTS = 4
NX = 1024
LIBRARY = 64
N_TILE = 64


def touch_ends(values, stream_key, low, high):
    longest = values.shape.index(max(values.shape))
    spots = []
    for shift in (0, 1):
        where = [jax.random.randint(jax.random.fold_in(stream_key, axis), (), 0, length) for axis, length in enumerate(values.shape)]
        where[longest] = (where[longest] + shift) % values.shape[longest]
        spots.append(tuple(where))
    return values.at[spots[0]].set(low).at[spots[1]].set(high)


def block_levels(stream_key, extent, shards, least, high):
    loudness = 1.0
    for axis_at, parts in shards:
        steps = jax.random.uniform(jax.random.fold_in(jax.random.fold_in(stream_key, 6), axis_at), (parts,), jnp.float32, least / len(shards), high / len(shards))
        loudness = loudness * jnp.repeat(jnp.exp(steps), extent[axis_at] // parts).reshape((-1,) + (1,) * (len(extent) - 1 - axis_at))
    return loudness


def noise(stream_key, dims, scale, bound, split=(), kind=jnp.bfloat16):
    entries = jax.random.normal(stream_key, dims, jnp.float32) * scale
    if len(split) > 0:
        entries = block_levels(stream_key, dims, split, -0.22, 0.18) * entries
    return jnp.clip(entries, min=-bound, max=bound).astype(kind)


def setup_inputs(seed: int = 0) -> dict:
    keys = jax.random.split(jax.random.key(seed), 6)
    return {
        "tomogram": noise(keys[0], (NX, LY, LZ), 1.0, 6.0, ((0, 64),)),
        "templates": noise(keys[1], (LIBRARY, TS, TS, TS), 1.0, 6.0, ((0, 64),)),
        "owners": jax.random.randint(keys[2], (STEPS,), 0, LIBRARY).astype(jnp.int32),
        "orient_ids": touch_ends(jax.random.randint(keys[3], (STEPS, ORIENTS), 0, 24), jax.random.fold_in(keys[3], 1), 0, 23).astype(jnp.int32),
        "slice_mask": touch_ends((jax.random.randint(keys[4], (NX,), 0, 4) < 3).astype(jnp.int32), jax.random.fold_in(keys[4], 1), 0, 1),
    }


einsum_forms = ('xyz,xk->kyz', 'xyz,yk->xkz', 'xyz,zk->xyk')

def rotation_list():
    even_orders = [(0, 1, 2), (1, 2, 0), (2, 0, 1)]
    odd_orders = [(0, 2, 1), (2, 1, 0), (1, 0, 2)]
    even_flips = [(), (0, 1), (0, 2), (1, 2)]
    odd_flips = [(0,), (1,), (2,), (0, 1, 2)]
    combos = [(order, flips) for order in even_orders for flips in even_flips]
    return combos + [(order, flips) for order in odd_orders for flips in odd_flips]

def rotate(volume, index):

    def make(order, flips):

        def turned(block):
            moved = jnp.transpose(block, order)
            if len(flips) > 0:
                moved = jnp.flip(moved, flips)
            return moved
        return turned
    branches = [make(order, flips) for order, flips in rotation_list()]
    return lax.switch(index, branches, volume)

def dft_table(count_in, count_out, length):
    rows = jnp.arange(count_in, dtype=jnp.int32)[:, None]
    cols = jnp.arange(count_out, dtype=jnp.int32)[None, :]
    phase = rows * cols % length
    angle = phase.astype(jnp.float32) * jnp.float32(2.0 * math.pi / length)
    return (jnp.cos(angle).astype(jnp.bfloat16), jnp.sin(angle).astype(jnp.bfloat16))

def contract(data, table, axis):
    return jnp.einsum(einsum_forms[axis], data.astype(jnp.float32), table.astype(jnp.float32))

def real_forward(data, axis, count_out, length):
    cos_t, sin_t = dft_table(data.shape[axis], count_out, length)
    real = contract(data, cos_t, axis)
    imag = -contract(data, sin_t, axis)
    return (real.astype(jnp.bfloat16), imag.astype(jnp.bfloat16))

def complex_forward(real, imag, axis, count_out, length):
    cos_t, sin_t = dft_table(real.shape[axis], count_out, length)
    new_real = contract(real, cos_t, axis) + contract(imag, sin_t, axis)
    new_imag = contract(imag, cos_t, axis) - contract(real, sin_t, axis)
    return (new_real.astype(jnp.bfloat16), new_imag.astype(jnp.bfloat16))

def complex_inverse(real, imag, axis, count_out, length):
    cos_t, sin_t = dft_table(real.shape[axis], count_out, length)
    new_real = contract(real, cos_t, axis) - contract(imag, sin_t, axis)
    new_imag = contract(imag, cos_t, axis) + contract(real, sin_t, axis)
    return (new_real.astype(jnp.bfloat16), new_imag.astype(jnp.bfloat16))

def real_inverse(real, imag, axis, count_out, length):
    cos_t, sin_t = dft_table(real.shape[axis], count_out, length)
    return contract(real, cos_t, axis) - contract(imag, sin_t, axis)

def yz_spectrum(data):
    real, imag = real_forward(data, 2, data.shape[2], data.shape[2])
    return complex_forward(real, imag, 1, data.shape[1], data.shape[1])

def template_spectrum(turned, length, wide_y, wide_z):
    real, imag = real_forward(turned, 2, wide_z, wide_z)
    real, imag = complex_forward(real, imag, 1, wide_y, wide_y)
    return complex_forward(real, imag, 0, length, length)

def normalize(base):
    values = base.astype(jnp.float32)
    center = jnp.mean(values)
    spread = jnp.mean((values - center) * (values - center))
    return (values - center) * lax.rsqrt(spread + 1e-05)

def box_band(count_in, count_out, edge, period):
    rows = jnp.arange(count_in, dtype=jnp.int32)[:, None]
    cols = jnp.arange(count_out, dtype=jnp.int32)[None, :]
    offset = (rows - cols) % period
    return (offset < edge).astype(jnp.float32)

def box_sum(field, slab, edge):
    length, wide_y, wide_z = field.shape
    first = jnp.einsum(einsum_forms[0], field, box_band(length, slab, edge, length + slab), precision=lax.Precision.HIGHEST)
    second = jnp.einsum(einsum_forms[1], first, box_band(wide_y, wide_y, edge, wide_y), precision=lax.Precision.HIGHEST)
    return jnp.einsum(einsum_forms[2], second, box_band(wide_z, wide_z, edge, wide_z), precision=lax.Precision.HIGHEST)

def local_scale(extended, slab, edge):
    volume = float(edge * edge * edge)
    mean_t = box_sum(extended, slab, edge) / volume
    mean_sq = box_sum(extended * extended, slab, edge) / volume
    return lax.rsqrt(mean_sq - mean_t * mean_t + 1e-05) / jnp.float32(math.sqrt(volume))

def correlate(tomo_r, tomo_i, temp_r, temp_i, slab):
    length, wide_y, wide_z = tomo_r.shape
    slab_r = tomo_r.astype(jnp.float32)
    slab_i = tomo_i.astype(jnp.float32)
    spec_r = temp_r.astype(jnp.float32)
    spec_i = temp_i.astype(jnp.float32)
    prod_r = (slab_r * spec_r + slab_i * spec_i).astype(jnp.bfloat16)
    prod_i = (slab_i * spec_r - slab_r * spec_i).astype(jnp.bfloat16)
    real, imag = complex_inverse(prod_r, prod_i, 0, slab, length)
    real, imag = complex_inverse(real, imag, 1, wide_y, wide_y)
    result = real_inverse(real, imag, 2, wide_z, wide_z)
    return result / float(length * wide_y * wide_z)

def reference(tomogram, templates, owners, orient_ids, slice_mask):
    length = CX + TS - 1
    spectra_r = []
    spectra_i = []
    for step in range(STEPS):
        base = lax.dynamic_index_in_dim(templates, owners[step], 0, keepdims=False)
        prepared = normalize(base)
        for orient in range(ORIENTS):
            turned = rotate(prepared, orient_ids[step, orient]).astype(jnp.bfloat16)
            temp_r, temp_i = template_spectrum(turned, length, LY, LZ)
            spectra_r.append(temp_r)
            spectra_i.append(temp_i)
    stack_r = jnp.stack(spectra_r)
    stack_i = jnp.stack(spectra_i)
    zeros = jnp.zeros((TS - 1, LY, LZ), jnp.bfloat16)
    padded = jnp.concatenate([tomogram, zeros], axis=0)
    yz_r, yz_i = yz_spectrum(padded)

    def one_slab(index):
        start = (index * CX).astype(jnp.int32)
        part_r = lax.dynamic_slice_in_dim(yz_r, start, length, 0)
        part_i = lax.dynamic_slice_in_dim(yz_i, start, length, 0)
        extended = lax.dynamic_slice_in_dim(padded, start, length, 0)
        tomo_r, tomo_i = complex_forward(part_r, part_i, 0, length, length)
        factor = local_scale(extended.astype(jnp.float32), CX, TS)

        def fold(best, spectra):
            score = correlate(tomo_r, tomo_i, spectra[0], spectra[1], CX) * factor
            return (jnp.maximum(best, score), None)
        init = jnp.full((CX, LY, LZ), -jnp.inf, jnp.float32)
        best, unused = lax.scan(fold, init, (stack_r, stack_i))
        return best
    slabs = lax.map(one_slab, jnp.arange(N_TILE, dtype=jnp.int32))
    best = slabs.reshape(NX, LY, LZ)
    return best * slice_mask.astype(jnp.float32)[:, None, None]
```

```python
import math

import jax
import jax.numpy as jnp
import numpy as np
from jax import lax
from jax.experimental import pallas as pl
from jax.experimental.pallas import tpu as pltpu
from jax.sharding import Mesh
from jax.sharding import PartitionSpec as P


TILE = ("tile_0", "tile_1", "tile_2")
EDGE = 32
SLAB = 16
WIDE = 128
LENGTH = 48
HALF = LENGTH // 2
FREQS = HALF + 1
PAIRS = (FREQS + 1) // 2
BF16 = jnp.bfloat16
F32 = jnp.float32


def plus(a, b):
    if a is None:
        return b
    return a if b is None else a + b


def minus(a, b):
    if b is None:
        return a
    return -b if a is None else a - b


def weighted(terms):
    total = None
    for value, weight in terms:
        if value is None or abs(weight) < 1e-9:
            continue
        if abs(abs(weight) - 1.0) < 1e-9:
            part = value
        else:
            part = value * jnp.float32(abs(weight))
        if weight > 0:
            total = plus(total, part)
        else:
            total = minus(total, part)
    return total


def cosine(j, k, n):
    return math.cos(2.0 * math.pi * ((j * k) % n) / n)


def sine(j, k, n):
    return math.sin(2.0 * math.pi * ((j * k) % n) / n)


def cos_forward(n, e):
    half = n // 2
    if n % 4:
        return [weighted([(e[j], cosine(j, k, n)) for j in range(half + 1)]) for k in range(half + 1)]
    even = cos_forward(half, e[0::2])
    out = [None] * (half + 1)
    for k in range(n // 4 + 1):
        odd = weighted([(e[j], cosine(j, k, n)) for j in range(1, half, 2)])
        out[k] = plus(even[k], odd)
        if k < n // 4:
            out[half - k] = minus(even[k], odd)
    return out


def sin_forward(n, o):
    half = n // 2
    if n % 4:
        return [weighted([(o[j], sine(j, k, n)) for j in range(1, half)]) if k % half else None for k in range(half + 1)]
    even = sin_forward(half, o[0::2])
    out = [None] * (half + 1)
    for k in range(1, n // 4 + 1):
        odd = weighted([(o[j], sine(j, k, n)) for j in range(1, half, 2)])
        out[k] = plus(even[k], odd) if k < n // 4 else odd
        if k < n // 4:
            out[half - k] = minus(odd, even[k])
    return out


def cos_inverse(n, f, wanted):
    half, quarter = n // 2, n // 4
    if n % 4:
        return {x: weighted([(f[k], cosine(k, x, n)) for k in range(half + 1)]) for x in wanted}
    out = {}
    evens = [x // 2 for x in wanted if x % 2 == 0]
    odds = [x for x in wanted if x % 2]
    if odds:
        q = [minus(f[k], f[half - k]) for k in range(quarter)]
        for x in odds:
            out[x] = weighted([(q[k], cosine(k, x, n)) for k in range(quarter)])
    if evens:
        p = [plus(f[k], f[half - k]) for k in range(quarter)] + [f[quarter]]
        for x, value in cos_inverse(half, p, evens).items():
            out[2 * x] = value
    return out


def sin_inverse(n, g, wanted):
    half, quarter = n // 2, n // 4
    if n % 4:
        return {x: weighted([(g[k], sine(k, x, n)) for k in range(1, half)]) for x in wanted}
    out = {}
    evens = [x // 2 for x in wanted if x % 2 == 0]
    odds = [x for x in wanted if x % 2]
    if odds:
        t = [None] + [plus(g[k], g[half - k]) for k in range(1, quarter)] + [g[quarter]]
        for x in odds:
            out[x] = weighted([(t[k], sine(k, x, n)) for k in range(1, quarter + 1)])
    if evens:
        r = [None] + [minus(g[k], g[half - k]) for k in range(1, quarter)] + [None]
        for x, value in sin_inverse(half, r, evens).items():
            out[2 * x] = value
    return out


def slices_forward(s):
    e = [s[0]] + [plus(s[j], s[LENGTH - j]) for j in range(1, HALF)] + [s[HALF]]
    o = [None] + [minus(s[j], s[LENGTH - j]) for j in range(1, HALF)] + [None]
    return cos_forward(LENGTH, e), sin_forward(LENGTH, o)


def tables():
    def table(rows, cols):
        angle = (np.outer(np.arange(rows), np.arange(cols)) % WIDE).astype(np.float32)
        angle = angle * np.float32(2.0 * math.pi / WIDE)
        return np.cos(angle), np.sin(angle)

    c, s = table(WIDE, WIDE)
    first = np.block([[c, -s], [s, c]])
    second = np.block([[c, s], [-s, c]])
    small_z, small_y = [], []
    for flip in (False, True):
        c, s = table(EDGE, WIDE)
        if flip:
            c, s = c[::-1], s[::-1]
        small_z.append(np.block([[c, -s], [s, c]]))
        small_y.append(np.block([[c.T, s.T], [-s.T, c.T]]))
    return [
        jnp.asarray(t.astype(np.float32)).astype(BF16)
        for t in (first, second, np.stack(small_z), np.stack(small_y))
    ]


def dot(a, b):
    return jnp.dot(a, b, preferred_element_type=F32)


def spot(k):
    return k // 2, (k % 2) * WIDE


def slab_kernel(core_ref, tomo_ref, own_ref, other_ref, first_ref, second_ref, spec_ref, factor_ref,
                halo_ref, x_ref, z_ref, sum_ref, square_ref):
    core = core_ref[0]
    for hop in range(2):
        halo_ref[pl.ds(hop * SLAB + 8 * core, 8)] = own_ref[hop]
        halo_ref[pl.ds(hop * SLAB + 8 * (1 - core), 8)] = other_ref[hop]

    def rows(step, carry):
        at = pl.ds(pl.multiple_of(step * 16, 16), 16)
        s = [tomo_ref[j, at, :] if j < SLAB else halo_ref[j - SLAB, at, :] for j in range(LENGTH)]
        s = [value.astype(F32) for value in s]
        s[LENGTH - 1] = None
        real, imag = slices_forward(s)
        for k in range(FREQS):
            x_ref[k, at, :WIDE] = real[k].astype(BF16)
            if imag[k] is None:
                x_ref[k, at, WIDE:] = jnp.zeros((16, WIDE), BF16)
            else:
                x_ref[k, at, WIDE:] = (-imag[k]).astype(BF16)
        return carry

    lax.fori_loop(0, WIDE // 16, rows, 0)

    def windows(step, carry):
        at = pl.ds(pl.multiple_of(step * 16, 16), 16)
        s = [tomo_ref[j, at, :] if j < SLAB else halo_ref[j - SLAB, at, :] for j in range(LENGTH - 1)]
        s = [value.astype(F32) for value in s]
        for target, field in ((sum_ref, s), (square_ref, [value * value for value in s])):
            for reach in (1, 2, 4, 8, 16):
                field = [field[j] + field[j + reach] for j in range(len(field) - reach)]
            for x in range(SLAB):
                target[x, at, :] = field[x]
        return carry

    lax.fori_loop(0, WIDE // 16, windows, 0)

    for k in range(FREQS):
        pair, lane = spot(k)
        moved = dot(x_ref[k], first_ref[...]).astype(BF16)
        z_ref[pair, :WIDE, lane:lane + WIDE] = moved[:, :WIDE]
        z_ref[pair, WIDE:, lane:lane + WIDE] = moved[:, WIDE:]
    for pair in range(PAIRS):
        width = WIDE if pair == PAIRS - 1 else 2 * WIDE
        spec_ref[pair, :, :width] = dot(second_ref[...], z_ref[pair, :, :width]).astype(BF16)
        if width == WIDE:
            spec_ref[pair, :, WIDE:] = jnp.zeros((2 * WIDE, WIDE), BF16)

    volume = float(EDGE**3)

    def boxed(field):
        for axis in (0, 1):
            for reach in (1, 2, 4, 8, 16):
                field = field + pltpu.roll(field, WIDE - reach, axis)
        return field / volume

    def scale(x, carry):
        mean_t = boxed(sum_ref[x])
        mean_sq = boxed(square_ref[x])
        root = lax.rsqrt(mean_sq - mean_t * mean_t + 1e-05) / jnp.float32(math.sqrt(volume))
        factor_ref[x] = root * jnp.float32(2.0 / (LENGTH * WIDE * WIDE))
        return carry

    lax.fori_loop(0, SLAB, scale, 0)


def slab_call(core, tomogram, own, other, first, second):
    vmem = pl.BlockSpec(memory_space=pltpu.VMEM)
    return pl.pallas_call(
        slab_kernel,
        out_shape=(
            jax.ShapeDtypeStruct((PAIRS, 2 * WIDE, 2 * WIDE), BF16),
            jax.ShapeDtypeStruct((SLAB, WIDE, WIDE), F32),
        ),
        in_specs=[pl.BlockSpec(memory_space=pltpu.SMEM)] + [vmem] * 5,
        out_specs=(vmem, vmem),
        scratch_shapes=[
            pltpu.VMEM((2 * SLAB, WIDE, WIDE), BF16),
            pltpu.VMEM((FREQS, WIDE, 2 * WIDE), BF16),
            pltpu.VMEM((PAIRS, 2 * WIDE, 2 * WIDE), BF16),
            pltpu.VMEM((SLAB, WIDE, WIDE), F32),
            pltpu.VMEM((SLAB, WIDE, WIDE), F32),
        ],
        compiler_params=pltpu.CompilerParams(vmem_limit_bytes=40 << 20),
        cost_estimate=pl.CostEstimate(flops=4_000_000_000, transcendentals=0, bytes_accessed=6_000_000),
        name="slab",
    )(core, tomogram, own, other, first, second)


def match_kernel(core_ref, orient_ref, own_ref, other_ref, spec_ref, factor_ref, first_ref, second_ref,
                 small_z_ref, small_y_ref, best_ref,
                 base_ref, cube_ref, cube_out_ref, packed_ref, a_ref, z_ref, p_ref, q_ref, f_ref, held_ref):
    step = pl.program_id(0)
    core = core_ref[0]

    @pl.when(step == 0)
    def _():
        for mine, half_ref in ((core, own_ref), (1 - core, other_ref)):
            values = half_ref[...].astype(F32)
            for group in range(4):
                start = pl.multiple_of((16 * mine + 4 * group) * EDGE, 128)
                base_ref[pl.ds(start, 4 * EDGE), :] = values[:, group * EDGE:(group + 1) * EDGE]
        values = base_ref[...]
        total = float(EDGE**3)
        center = jnp.sum(values) / total
        values = values - center
        spread = jnp.sum(values * values) / total
        base_ref[...] = (values * lax.rsqrt(spread + 1e-05)).astype(BF16).astype(F32)

    index = orient_ref[step]
    order = index // 4
    flips = index % 4
    odd_order = order >= 3
    turn_a = (order == 2) | (order == 3) | (order == 4)
    turn_b = (order == 1) | (order == 2) | (order == 4) | (order == 5)
    turn_c = (order == 1) | (order == 4)
    flip_y = flips % 2
    flip_z = flips // 2
    middle = ((flips == 1) | (flips == 2)).astype(jnp.int32)
    flip_x = jnp.where(odd_order, 1 - middle, middle)

    def swap_last(source, target):
        for a in range(EDGE):
            at = slice(a * EDGE, (a + 1) * EDGE)
            target[at, :] = source[at, :].T

    def copy(source, target):
        target[...] = source[...]

    @pl.when(turn_a)
    def _():
        swap_last(base_ref, cube_ref)

    @pl.when(jnp.logical_not(turn_a))
    def _():
        copy(base_ref, cube_ref)

    @pl.when(turn_b)
    def _():
        for b in range(EDGE):
            cube_out_ref[b * EDGE:(b + 1) * EDGE, :] = cube_ref[pl.ds(b, EDGE, stride=EDGE), :]

    @pl.when(jnp.logical_not(turn_b))
    def _():
        copy(cube_ref, cube_out_ref)

    @pl.when(turn_c)
    def _():
        swap_last(cube_out_ref, cube_ref)

    @pl.when(jnp.logical_not(turn_c))
    def _():
        copy(cube_out_ref, cube_ref)

    for x in range(EDGE):
        tile = cube_ref[x * EDGE:(x + 1) * EDGE, :]
        packed_ref[x] = jnp.concatenate([tile[8 * g:8 * g + 8] for g in range(4)], axis=1)

    s = [None] * LENGTH
    for i in range(EDGE):
        s[i + SLAB // 2] = packed_ref[jnp.where(flip_x == 1, EDGE - 1 - i, i)]
    real, imag = slices_forward(s)
    for k in range(FREQS):
        share = 0.5 if k in (0, HALF) else 1.0
        for g in range(4):
            at = slice(k * EDGE + 8 * g, k * EDGE + 8 * g + 8)
            lanes = slice(g * EDGE, (g + 1) * EDGE)
            a_ref[at, :EDGE] = real[k][:, lanes] * jnp.float32(share)
            if imag[k] is None:
                a_ref[at, EDGE:2 * EDGE] = jnp.zeros((8, EDGE), F32)
            else:
                a_ref[at, EDGE:2 * EDGE] = -imag[k][:, lanes]

    moved = dot(a_ref[...].astype(BF16), small_z_ref[flip_z]).astype(BF16)
    for k in range(FREQS):
        pair, lane = spot(k)
        part = moved[k * EDGE:(k + 1) * EDGE]
        z_ref[pair, :EDGE, lane:lane + WIDE] = part[:, :WIDE]
        z_ref[pair, EDGE:, lane:lane + WIDE] = part[:, WIDE:]

    small_y = small_y_ref[flip_y]
    for pair in range(PAIRS):
        width = WIDE if pair == PAIRS - 1 else 2 * WIDE
        temp = dot(small_y, z_ref[pair, :, :width])
        slab = spec_ref[pair, :, :width].astype(F32)
        temp_r, temp_i = temp[:WIDE], temp[WIDE:]
        slab_r, slab_i = slab[:WIDE], slab[WIDE:]
        prod_r = (slab_r * temp_r + slab_i * temp_i).astype(BF16)
        prod_i = (slab_i * temp_r - slab_r * temp_i).astype(BF16)
        for part in range(width // WIDE):
            k = 2 * pair + part
            lanes = slice(part * WIDE, (part + 1) * WIDE)
            p_ref[k, :, :WIDE] = prod_r[:, lanes]
            p_ref[k, :, WIDE:] = prod_i[:, lanes]

    for k in range(FREQS):
        pair, lane = spot(k)
        moved = dot(p_ref[k], second_ref[...]).astype(BF16)
        q_ref[pair, :WIDE, lane:lane + WIDE] = moved[:, :WIDE]
        q_ref[pair, WIDE:, lane:lane + WIDE] = moved[:, WIDE:]
    for pair in range(PAIRS):
        width = WIDE if pair == PAIRS - 1 else 2 * WIDE
        f_ref[pair, :, :width] = dot(first_ref[...], q_ref[pair, :, :width])

    def scores(block, finish):
        at = pl.multiple_of(block * 8, 8)
        fr, fi = [], []
        for k in range(FREQS):
            pair, lane = spot(k)
            fr.append(f_ref[pair, pl.ds(at, 8), lane:lane + WIDE])
            fi.append(f_ref[pair, pl.ds(WIDE + at, 8), lane:lane + WIDE])
        reach = SLAB // 2
        even = cos_inverse(LENGTH, fr, list(range(reach + 1)))
        odd = sin_inverse(LENGTH, fi, list(range(1, reach + 1)))
        for x in range(SLAB):
            lag = x - reach
            if lag == 0:
                value = even[0]
            elif lag > 0:
                value = even[lag] - odd[lag]
            else:
                value = even[-lag] + odd[-lag]
            finish(x, pl.ds(at, 8), value * factor_ref[x, pl.ds(at, 8), :])

    @pl.when(step == 0)
    def _():
        def body(block, carry):
            def keep(x, at, value):
                held_ref[x, at, :] = value
            scores(block, keep)
            return carry
        lax.fori_loop(0, WIDE // 8, body, 0)

    @pl.when(step == 1)
    def _():
        def body(block, carry):
            def keep(x, at, value):
                held_ref[x, at, :] = jnp.maximum(held_ref[x, at, :], value)
            scores(block, keep)
            return carry
        lax.fori_loop(0, WIDE // 8, body, 0)
        best_ref[...] = held_ref[...].astype(BF16)


def match_call(core, orients, own, other, spec, factor, first, second, small_z, small_y):
    vmem = pl.BlockSpec(memory_space=pltpu.VMEM)
    smem = pl.BlockSpec(memory_space=pltpu.SMEM)
    cube = EDGE * EDGE
    return pl.pallas_call(
        match_kernel,
        grid=(2,),
        out_shape=jax.ShapeDtypeStruct((SLAB, WIDE, WIDE), BF16),
        in_specs=[smem, smem] + [vmem] * 8,
        out_specs=vmem,
        scratch_shapes=[
            pltpu.VMEM((cube, EDGE), F32),
            pltpu.VMEM((cube, EDGE), F32),
            pltpu.VMEM((cube, EDGE), F32),
            pltpu.VMEM((EDGE, 8, WIDE), F32),
            pltpu.VMEM((FREQS * EDGE, 2 * EDGE), F32),
            pltpu.VMEM((PAIRS, 2 * EDGE, 2 * WIDE), BF16),
            pltpu.VMEM((FREQS, WIDE, 2 * WIDE), BF16),
            pltpu.VMEM((PAIRS, 2 * WIDE, 2 * WIDE), BF16),
            pltpu.VMEM((PAIRS, 2 * WIDE, 2 * WIDE), F32),
            pltpu.VMEM((SLAB, WIDE, WIDE), F32),
        ],
        compiler_params=pltpu.CompilerParams(vmem_limit_bytes=40 << 20),
        cost_estimate=pl.CostEstimate(flops=8_000_000_000, transcendentals=0, bytes_accessed=6_000_000),
        name="match",
    )(core, orients, own, other, spec, factor, first, second, small_z, small_y)


def shifted(value, axis, by):
    length = lax.axis_size(axis)
    pairs = [(i, i + by) for i in range(length) if 0 <= i + by < length]
    return lax.ppermute(value, axis, pairs)


def swapped(value, axis):
    return lax.ppermute(value, axis, [(0, 1), (1, 0)])


def from_member(value, axis, root):
    length = lax.axis_size(axis)
    sent = jnp.broadcast_to(value[None], (length, *value.shape))
    got = lax.all_to_all(sent, axis, 0, 0, tiled=True)
    return lax.dynamic_index_in_dim(got, root, 0, keepdims=False)


def shards(tomogram, templates, owners, orient_ids, slice_mask):
    core = lax.axis_index("core")
    core_arg = core.astype(jnp.int32)[None]
    first, second, small_z, small_y = tables()

    half = lax.dynamic_slice_in_dim(templates[0], 16 * core, 16, 0)
    half = jnp.concatenate([half[4 * g:4 * g + 4].reshape(4 * EDGE, EDGE) for g in range(4)], axis=1)
    plane = lax.axis_size(("tile_1", "tile_2"))
    half = from_member(half, "tile_0", owners[0] // plane)
    half = from_member(half, ("tile_1", "tile_2"), owners[0] % plane)
    other_half = swapped(half, "core")

    slices = lax.dynamic_slice_in_dim(tomogram, 8 * core, 8, 0)
    halo = jnp.stack([shifted(slices, TILE, -1), shifted(slices, TILE, -2)])
    other_halo = swapped(halo, "core")
    spec, factor = slab_call(core_arg, tomogram, halo, other_halo, first, second)

    own_id = orient_ids[0]
    orients = jnp.concatenate([own_id, swapped(own_id, "far")])
    best = match_call(
        core_arg, orients, half, other_half, spec, factor, first, second, small_z, small_y
    )
    best = jnp.maximum(best, swapped(best, "core"))
    return best.astype(F32) * slice_mask.astype(F32)[:, None, None]


def solution(mesh):
    torus = Mesh(
        mesh.devices.reshape(8, 4, 2, 2, 2), ("tile_0", "tile_1", "tile_2", "far", "core")
    )
    in_specs = (P(TILE, None, None), P(TILE, None, None, None), P(), P(None, ("far", "core")), P(TILE))
    out_specs = P(TILE, None, None)
    return jax.shard_map(
        shards, mesh=torus, in_specs=in_specs, out_specs=out_specs, check_vma=False
    )
```

```python
import itertools
import math

import jax
import jax.numpy as jnp
import numpy as np
from jax import lax
from jax.experimental import pallas as pl
from jax.experimental.pallas import tpu as pltpu
from jax.sharding import Mesh
from jax.sharding import PartitionSpec as P


TILE = ("tile_0", "tile_1", "tile_2")
EDGE = 32
SLAB = 16
WIDE = 128
LENGTH = 48
HALF = LENGTH // 2
FREQS = HALF + 1
PAIRS = (FREQS + 1) // 2
BF16 = jnp.bfloat16
F32 = jnp.float32


def plus(a, b):
    if a is None:
        return b
    return a if b is None else a + b


def minus(a, b):
    if b is None:
        return a
    return -b if a is None else a - b


def weighted(terms):
    total = None
    for value, weight in terms:
        if value is None or abs(weight) < 1e-9:
            continue
        if abs(abs(weight) - 1.0) < 1e-9:
            part = value
        else:
            part = value * jnp.float32(abs(weight))
        if weight > 0:
            total = plus(total, part)
        else:
            total = minus(total, part)
    return total


def cosine(j, k, n):
    return math.cos(2.0 * math.pi * ((j * k) % n) / n)


def sine(j, k, n):
    return math.sin(2.0 * math.pi * ((j * k) % n) / n)


def cos_forward(n, e):
    half = n // 2
    if n % 4:
        return [weighted([(e[j], cosine(j, k, n)) for j in range(half + 1)]) for k in range(half + 1)]
    even = cos_forward(half, e[0::2])
    out = [None] * (half + 1)
    for k in range(n // 4 + 1):
        odd = weighted([(e[j], cosine(j, k, n)) for j in range(1, half, 2)])
        out[k] = plus(even[k], odd)
        if k < n // 4:
            out[half - k] = minus(even[k], odd)
    return out


def sin_forward(n, o):
    half = n // 2
    if n % 4:
        return [weighted([(o[j], sine(j, k, n)) for j in range(1, half)]) if k % half else None for k in range(half + 1)]
    even = sin_forward(half, o[0::2])
    out = [None] * (half + 1)
    for k in range(1, n // 4 + 1):
        odd = weighted([(o[j], sine(j, k, n)) for j in range(1, half, 2)])
        out[k] = plus(even[k], odd) if k < n // 4 else odd
        if k < n // 4:
            out[half - k] = minus(odd, even[k])
    return out


def cos_inverse(n, f, wanted):
    half, quarter = n // 2, n // 4
    if n % 4:
        return {x: weighted([(f[k], cosine(k, x, n)) for k in range(half + 1)]) for x in wanted}
    out = {}
    evens = [x // 2 for x in wanted if x % 2 == 0]
    odds = [x for x in wanted if x % 2]
    if odds:
        q = [minus(f[k], f[half - k]) for k in range(quarter)]
        for x in odds:
            out[x] = weighted([(q[k], cosine(k, x, n)) for k in range(quarter)])
    if evens:
        p = [plus(f[k], f[half - k]) for k in range(quarter)] + [f[quarter]]
        for x, value in cos_inverse(half, p, evens).items():
            out[2 * x] = value
    return out


def sin_inverse(n, g, wanted):
    half, quarter = n // 2, n // 4
    if n % 4:
        return {x: weighted([(g[k], sine(k, x, n)) for k in range(1, half)]) for x in wanted}
    out = {}
    evens = [x // 2 for x in wanted if x % 2 == 0]
    odds = [x for x in wanted if x % 2]
    if odds:
        t = [None] + [plus(g[k], g[half - k]) for k in range(1, quarter)] + [g[quarter]]
        for x in odds:
            out[x] = weighted([(t[k], sine(k, x, n)) for k in range(1, quarter + 1)])
    if evens:
        r = [None] + [minus(g[k], g[half - k]) for k in range(1, quarter)] + [None]
        for x, value in sin_inverse(half, r, evens).items():
            out[2 * x] = value
    return out


def slices_forward(s):
    e = [s[0]] + [plus(s[j], s[LENGTH - j]) for j in range(1, HALF)] + [s[HALF]]
    o = [None] + [minus(s[j], s[LENGTH - j]) for j in range(1, HALF)] + [None]
    return cos_forward(LENGTH, e), sin_forward(LENGTH, o)


def tables():
    def table(rows, cols):
        angle = (np.outer(np.arange(rows), np.arange(cols)) % WIDE).astype(np.float32)
        angle = angle * np.float32(2.0 * math.pi / WIDE)
        return np.cos(angle), np.sin(angle)

    c, s = table(WIDE, WIDE)
    first = np.block([[c, -s], [s, c]])
    second = np.block([[c, s], [-s, c]])
    small_z, small_y = [], []
    for flip in (False, True):
        c, s = table(EDGE, WIDE)
        if flip:
            c, s = c[::-1], s[::-1]
        small_z.append(np.block([[c, -s], [s, c]]))
        small_y.append(np.block([[c.T, s.T], [-s.T, c.T]]))
    return [
        jnp.asarray(t.astype(np.float32)).astype(BF16)
        for t in (first, second, np.stack(small_z), np.stack(small_y))
    ]


def dot(a, b):
    return jnp.dot(a, b, preferred_element_type=F32)


def spot(k):
    return k // 2, (k % 2) * WIDE


def fill_halo(core_ref, own_ref, other_ref, halo_ref):
    core = core_ref[0]
    for hop in range(2):
        halo_ref[pl.ds(hop * SLAB + 8 * core, 8)] = own_ref[hop]
        halo_ref[pl.ds(hop * SLAB + 8 * (1 - core), 8)] = other_ref[hop]


def load_rows(tomo_ref, halo_ref, at):
    s = [tomo_ref[j, at, :] if j < SLAB else halo_ref[j - SLAB, at, :] for j in range(LENGTH - 1)]
    return [value.astype(F32) for value in s]


def spectrum_kernel(core_ref, tomo_ref, own_ref, other_ref, first_ref, second_ref, spec_ref,
                    halo_ref, x_ref, z_ref):
    fill_halo(core_ref, own_ref, other_ref, halo_ref)

    def rows(step, carry):
        at = pl.ds(pl.multiple_of(step * 16, 16), 16)
        real, imag = slices_forward(load_rows(tomo_ref, halo_ref, at) + [None])
        for k in range(FREQS):
            x_ref[k, at, :WIDE] = real[k].astype(BF16)
            if imag[k] is None:
                x_ref[k, at, WIDE:] = jnp.zeros((16, WIDE), BF16)
            else:
                x_ref[k, at, WIDE:] = (-imag[k]).astype(BF16)
        return carry

    lax.fori_loop(0, WIDE // 16, rows, 0)

    for k in range(FREQS):
        pair, lane = spot(k)
        moved = dot(x_ref[k], first_ref[...]).astype(BF16)
        z_ref[pair, :WIDE, lane:lane + WIDE] = moved[:, :WIDE]
        z_ref[pair, WIDE:, lane:lane + WIDE] = moved[:, WIDE:]
    for pair in range(PAIRS):
        width = WIDE if pair == PAIRS - 1 else 2 * WIDE
        spec_ref[pair, :, :width] = dot(second_ref[...], z_ref[pair, :, :width]).astype(BF16)
        if width == WIDE:
            spec_ref[pair, :, WIDE:] = jnp.zeros((2 * WIDE, WIDE), BF16)


def factor_kernel(core_ref, tomo_ref, own_ref, other_ref, factor_ref, halo_ref, sum_ref, square_ref):
    fill_halo(core_ref, own_ref, other_ref, halo_ref)

    def windows(step, carry):
        at = pl.ds(pl.multiple_of(step * 16, 16), 16)
        s = load_rows(tomo_ref, halo_ref, at)
        for target, field in ((sum_ref, s), (square_ref, [value * value for value in s])):
            for reach in (1, 2, 4, 8, 16):
                field = [field[j] + field[j + reach] for j in range(len(field) - reach)]
            for x in range(SLAB):
                target[x, at, :] = field[x]
        return carry

    lax.fori_loop(0, WIDE // 16, windows, 0)

    volume = float(EDGE**3)

    def boxed(field):
        for axis in (0, 1):
            for reach in (1, 2, 4, 8, 16):
                field = field + pltpu.roll(field, WIDE - reach, axis)
        return field / volume

    def scale(x, carry):
        mean_t = boxed(sum_ref[x])
        mean_sq = boxed(square_ref[x])
        root = lax.rsqrt(mean_sq - mean_t * mean_t + 1e-05) / jnp.float32(math.sqrt(volume))
        factor_ref[x] = root * jnp.float32(2.0 / (LENGTH * WIDE * WIDE))
        return carry

    lax.fori_loop(0, SLAB, scale, 0)


def spectrum_call(core, tomogram, own, other, first, second):
    vmem = pl.BlockSpec(memory_space=pltpu.VMEM)
    return pl.pallas_call(
        spectrum_kernel,
        out_shape=jax.ShapeDtypeStruct((PAIRS, 2 * WIDE, 2 * WIDE), BF16),
        in_specs=[pl.BlockSpec(memory_space=pltpu.SMEM)] + [vmem] * 5,
        out_specs=vmem,
        scratch_shapes=[
            pltpu.VMEM((2 * SLAB, WIDE, WIDE), BF16),
            pltpu.VMEM((FREQS, WIDE, 2 * WIDE), BF16),
            pltpu.VMEM((PAIRS, 2 * WIDE, 2 * WIDE), BF16),
        ],
        compiler_params=pltpu.CompilerParams(vmem_limit_bytes=40 << 20),
        cost_estimate=pl.CostEstimate(flops=4_000_000_000, transcendentals=0, bytes_accessed=6_000_000),
        name="spectrum",
    )(core, tomogram, own, other, first, second)


def factor_call(core, tomogram, own, other):
    vmem = pl.BlockSpec(memory_space=pltpu.VMEM)
    return pl.pallas_call(
        factor_kernel,
        out_shape=jax.ShapeDtypeStruct((SLAB, WIDE, WIDE), F32),
        in_specs=[pl.BlockSpec(memory_space=pltpu.SMEM)] + [vmem] * 3,
        out_specs=vmem,
        scratch_shapes=[
            pltpu.VMEM((2 * SLAB, WIDE, WIDE), BF16),
            pltpu.VMEM((SLAB, WIDE, WIDE), F32),
            pltpu.VMEM((SLAB, WIDE, WIDE), F32),
        ],
        compiler_params=pltpu.CompilerParams(vmem_limit_bytes=40 << 20),
        cost_estimate=pl.CostEstimate(flops=4_000_000_000, transcendentals=0, bytes_accessed=6_000_000),
        name="factor",
    )(core, tomogram, own, other)


def prep_kernel(core_ref, tomo_ref, temp_ref, slices_ref, packed_ref):
    slices_ref[...] = tomo_ref[...]
    values = temp_ref[0].astype(F32).reshape(16 * EDGE, EDGE)
    rows = 4 * EDGE
    packed = jnp.concatenate([values[g * rows:(g + 1) * rows] for g in range(4)], axis=1).astype(BF16)
    for member in range(packed_ref.shape[0]):
        packed_ref[member] = packed


def prep_call(core, tomogram, templates, members):
    return pl.pallas_call(
        prep_kernel,
        out_shape=(
            jax.ShapeDtypeStruct((SLAB // 2, WIDE, WIDE), BF16),
            jax.ShapeDtypeStruct((members, WIDE, WIDE), BF16),
        ),
        grid_spec=pltpu.PrefetchScalarGridSpec(
            num_scalar_prefetch=1,
            grid=(1,),
            in_specs=[
                pl.BlockSpec((SLAB // 2, WIDE, WIDE), lambda i, core: (core[0], 0, 0)),
                pl.BlockSpec((1, EDGE // 2, EDGE, EDGE), lambda i, core: (0, core[0], 0, 0)),
            ],
            out_specs=(
                pl.BlockSpec((SLAB // 2, WIDE, WIDE), lambda i, core: (0, 0, 0)),
                pl.BlockSpec((members, WIDE, WIDE), lambda i, core: (0, 0, 0)),
            ),
        ),
        name="prep",
    )(core, tomogram, templates)


def match_kernel(core_ref, orient_ref, own_ref, other_ref, spec_ref, factor_ref, first_ref, second_ref,
                 small_z_ref, small_y_ref, best_ref,
                 base_ref, cube_ref, cube_out_ref, packed_ref, a_ref, z_ref, p_ref, q_ref, f_ref, held_ref):
    step = pl.program_id(0)
    core = core_ref[0]

    @pl.when(step == 0)
    def _():
        for mine, half_ref in ((core, own_ref), (1 - core, other_ref)):
            values = half_ref[...].astype(F32)
            for group in range(4):
                start = pl.multiple_of((16 * mine + 4 * group) * EDGE, 128)
                base_ref[pl.ds(start, 4 * EDGE), :] = values[:, group * EDGE:(group + 1) * EDGE]
        values = base_ref[...]
        total = float(EDGE**3)
        center = jnp.sum(values) / total
        values = values - center
        spread = jnp.sum(values * values) / total
        base_ref[...] = (values * lax.rsqrt(spread + 1e-05)).astype(BF16).astype(F32)

    index = orient_ref[step]
    order = index // 4
    flips = index % 4
    odd_order = order >= 3
    turn_a = (order == 2) | (order == 3) | (order == 4)
    turn_b = (order == 1) | (order == 2) | (order == 4) | (order == 5)
    turn_c = (order == 1) | (order == 4)
    flip_y = flips % 2
    flip_z = flips // 2
    middle = ((flips == 1) | (flips == 2)).astype(jnp.int32)
    flip_x = jnp.where(odd_order, 1 - middle, middle)

    def swap_last(source, target):
        for a in range(EDGE):
            at = slice(a * EDGE, (a + 1) * EDGE)
            target[at, :] = source[at, :].T

    def copy(source, target):
        target[...] = source[...]

    @pl.when(turn_a)
    def _():
        swap_last(base_ref, cube_ref)

    @pl.when(jnp.logical_not(turn_a))
    def _():
        copy(base_ref, cube_ref)

    @pl.when(turn_b)
    def _():
        for b in range(EDGE):
            cube_out_ref[b * EDGE:(b + 1) * EDGE, :] = cube_ref[pl.ds(b, EDGE, stride=EDGE), :]

    @pl.when(jnp.logical_not(turn_b))
    def _():
        copy(cube_ref, cube_out_ref)

    @pl.when(turn_c)
    def _():
        swap_last(cube_out_ref, cube_ref)

    @pl.when(jnp.logical_not(turn_c))
    def _():
        copy(cube_out_ref, cube_ref)

    for x in range(EDGE):
        tile = cube_ref[x * EDGE:(x + 1) * EDGE, :]
        packed_ref[x] = jnp.concatenate([tile[8 * g:8 * g + 8] for g in range(4)], axis=1)

    s = [None] * LENGTH
    for i in range(EDGE):
        s[i + SLAB // 2] = packed_ref[jnp.where(flip_x == 1, EDGE - 1 - i, i)]
    real, imag = slices_forward(s)
    for k in range(FREQS):
        share = 0.5 if k in (0, HALF) else 1.0
        for g in range(4):
            at = slice(k * EDGE + 8 * g, k * EDGE + 8 * g + 8)
            lanes = slice(g * EDGE, (g + 1) * EDGE)
            a_ref[at, :EDGE] = real[k][:, lanes] * jnp.float32(share)
            if imag[k] is None:
                a_ref[at, EDGE:2 * EDGE] = jnp.zeros((8, EDGE), F32)
            else:
                a_ref[at, EDGE:2 * EDGE] = -imag[k][:, lanes]

    moved = dot(a_ref[...].astype(BF16), small_z_ref[flip_z]).astype(BF16)
    for k in range(FREQS):
        pair, lane = spot(k)
        part = moved[k * EDGE:(k + 1) * EDGE]
        z_ref[pair, :EDGE, lane:lane + WIDE] = part[:, :WIDE]
        z_ref[pair, EDGE:, lane:lane + WIDE] = part[:, WIDE:]

    small_y = small_y_ref[flip_y]
    for pair in range(PAIRS):
        width = WIDE if pair == PAIRS - 1 else 2 * WIDE
        temp = dot(small_y, z_ref[pair, :, :width])
        slab = spec_ref[pair, :, :width].astype(F32)
        temp_r, temp_i = temp[:WIDE], temp[WIDE:]
        slab_r, slab_i = slab[:WIDE], slab[WIDE:]
        prod_r = (slab_r * temp_r + slab_i * temp_i).astype(BF16)
        prod_i = (slab_i * temp_r - slab_r * temp_i).astype(BF16)
        for part in range(width // WIDE):
            k = 2 * pair + part
            lanes = slice(part * WIDE, (part + 1) * WIDE)
            p_ref[k, :, :WIDE] = prod_r[:, lanes]
            p_ref[k, :, WIDE:] = prod_i[:, lanes]

    for k in range(FREQS):
        pair, lane = spot(k)
        moved = dot(p_ref[k], second_ref[...]).astype(BF16)
        q_ref[pair, :WIDE, lane:lane + WIDE] = moved[:, :WIDE]
        q_ref[pair, WIDE:, lane:lane + WIDE] = moved[:, WIDE:]
    for pair in range(PAIRS):
        width = WIDE if pair == PAIRS - 1 else 2 * WIDE
        f_ref[pair, :, :width] = dot(first_ref[...], q_ref[pair, :, :width])

    def scores(block, finish):
        at = pl.multiple_of(block * 8, 8)
        fr, fi = [], []
        for k in range(FREQS):
            pair, lane = spot(k)
            fr.append(f_ref[pair, pl.ds(at, 8), lane:lane + WIDE])
            fi.append(f_ref[pair, pl.ds(WIDE + at, 8), lane:lane + WIDE])
        reach = SLAB // 2
        even = cos_inverse(LENGTH, fr, list(range(reach + 1)))
        odd = sin_inverse(LENGTH, fi, list(range(1, reach + 1)))
        for x in range(SLAB):
            lag = x - reach
            if lag == 0:
                value = even[0]
            elif lag > 0:
                value = even[lag] - odd[lag]
            else:
                value = even[-lag] + odd[-lag]
            finish(x, pl.ds(at, 8), value * factor_ref[x, pl.ds(at, 8), :])

    @pl.when(step == 0)
    def _():
        def body(block, carry):
            def keep(x, at, value):
                held_ref[x, at, :] = value

            scores(block, keep)
            return carry

        lax.fori_loop(0, WIDE // 8, body, 0)

    @pl.when(step == 1)
    def _():
        def body(block, carry):
            def keep(x, at, value):
                held_ref[x, at, :] = jnp.maximum(held_ref[x, at, :], value)

            scores(block, keep)
            return carry

        lax.fori_loop(0, WIDE // 8, body, 0)
        best_ref[...] = held_ref[...].astype(BF16)


def match_call(core, orients, own, other, spec, factor, first, second, small_z, small_y):
    vmem = pl.BlockSpec(memory_space=pltpu.VMEM)
    smem = pl.BlockSpec(memory_space=pltpu.SMEM)
    cube = EDGE * EDGE
    return pl.pallas_call(
        match_kernel,
        grid=(2,),
        out_shape=jax.ShapeDtypeStruct((SLAB, WIDE, WIDE), BF16),
        in_specs=[smem, smem] + [vmem] * 8,
        out_specs=vmem,
        scratch_shapes=[
            pltpu.VMEM((cube, EDGE), F32),
            pltpu.VMEM((cube, EDGE), F32),
            pltpu.VMEM((cube, EDGE), F32),
            pltpu.VMEM((EDGE, 8, WIDE), F32),
            pltpu.VMEM((FREQS * EDGE, 2 * EDGE), F32),
            pltpu.VMEM((PAIRS, 2 * EDGE, 2 * WIDE), BF16),
            pltpu.VMEM((FREQS, WIDE, 2 * WIDE), BF16),
            pltpu.VMEM((PAIRS, 2 * WIDE, 2 * WIDE), BF16),
            pltpu.VMEM((PAIRS, 2 * WIDE, 2 * WIDE), F32),
            pltpu.VMEM((SLAB, WIDE, WIDE), F32),
        ],
        compiler_params=pltpu.CompilerParams(vmem_limit_bytes=40 << 20),
        cost_estimate=pl.CostEstimate(flops=8_000_000_000, transcendentals=0, bytes_accessed=6_000_000),
        name="match",
    )(core, orients, own, other, spec, factor, first, second, small_z, small_y)


def shifted(value, axis, by):
    length = lax.axis_size(axis)
    pairs = [(i, i + by) for i in range(length) if 0 <= i + by < length]
    return lax.ppermute(value, axis, pairs)


def swapped(value, axis):
    return lax.ppermute(value, axis, [(0, 1), (1, 0)])


def by_offset(value, axes, offset):
    sizes = [lax.axis_size(axis) for axis in axes]

    def flat(spots):
        index = 0
        for spot_at, size in zip(spots, sizes):
            index = index * size + spot_at % size
        return index

    pairs = [
        (flat(spots), flat([at + by for at, by in zip(spots, offset)]))
        for spots in itertools.product(*[range(size) for size in sizes])
    ]
    return lax.ppermute(value, axes, pairs)


def shards(tomogram, templates, owners, orient_ids, slice_mask):
    core_arg = lax.axis_index("core").astype(jnp.int32)[None]
    first, second, small_z, small_y = tables()
    rows, columns = lax.axis_size("tile_1"), lax.axis_size("tile_2")
    members = lax.axis_size("tile_0")
    root_x = lax.rem(owners[0], columns)
    root_y = lax.rem(lax.div(owners[0], columns), rows)
    root_z = lax.div(owners[0], rows * columns)
    off_y = lax.rem(lax.axis_index("tile_1") + rows - root_y, rows)
    off_x = lax.rem(lax.axis_index("tile_2") + columns - root_x, columns)
    even_y = lax.rem(off_y, 2) == 0

    slices, sent = prep_call(core_arg, tomogram, templates, members)
    near = shifted(slices, TILE, -1)
    far = shifted(slices, TILE, -2)
    got = lax.all_to_all(sent, "tile_0", 0, 0, tiled=True)
    other_id = swapped(orient_ids[0], "far")
    half = lax.dynamic_index_in_dim(got, root_z, 0, keepdims=False)
    halo = jnp.stack([near, far])
    other_halo = swapped(halo, "core")

    axes = ("tile_1", "tile_2")
    half = jnp.where(off_y == 2, by_offset(half, axes, (2, 0)), half)
    from_y = by_offset(half, axes, (1, 0))
    from_x = by_offset(half, axes, (0, 1))
    from_both = by_offset(half, axes, (1, 1))
    half = jnp.where(
        off_x == 0,
        jnp.where(even_y, half, from_y),
        jnp.where(even_y, from_x, from_both),
    )
    other_half = swapped(half, "core")

    spec = spectrum_call(core_arg, tomogram, halo, other_halo, first, second)
    factor = factor_call(core_arg, tomogram, halo, other_halo)

    orients = jnp.concatenate([orient_ids[0], other_id])
    best = match_call(
        core_arg, orients, half, other_half, spec, factor, first, second, small_z, small_y
    )
    best = jnp.maximum(best, swapped(best, "core"))
    return best.astype(F32) * slice_mask.astype(F32)[:, None, None]


def solution(mesh):
    torus = Mesh(
        mesh.devices.reshape(8, 4, 2, 2, 2), ("tile_0", "tile_1", "tile_2", "far", "core")
    )
    in_specs = (P(TILE, None, None), P(TILE, None, None, None), P(), P(None, ("far", "core")), P(TILE))
    out_specs = P(TILE, None, None)
    return jax.shard_map(
        shards, mesh=torus, in_specs=in_specs, out_specs=out_specs, check_vma=False
    )
```

```python
import itertools
import math

import jax
import jax.numpy as jnp
import numpy as np
from jax import lax
from jax.experimental import pallas as pl
from jax.experimental.pallas import tpu as pltpu
from jax.sharding import Mesh
from jax.sharding import PartitionSpec as P


TILE = ("tile_0", "tile_1", "tile_2")
EDGE = 32
TAIL = 16
SLAB = 16
WIDE = 128
LENGTH = 48
HALF = LENGTH // 2
FREQS = HALF + 1
PAIRS = (FREQS + 1) // 2
BF16 = jnp.bfloat16
F32 = jnp.float32


def plus(a, b):
    if a is None:
        return b
    return a if b is None else a + b


def minus(a, b):
    if b is None:
        return a
    return -b if a is None else a - b


def weighted(terms):
    total = None
    for value, weight in terms:
        if value is None or abs(weight) < 1e-9:
            continue
        if abs(abs(weight) - 1.0) < 1e-9:
            part = value
        else:
            part = value * jnp.float32(abs(weight))
        if weight > 0:
            total = plus(total, part)
        else:
            total = minus(total, part)
    return total


def cosine(j, k, n):
    return math.cos(2.0 * math.pi * ((j * k) % n) / n)


def sine(j, k, n):
    return math.sin(2.0 * math.pi * ((j * k) % n) / n)


def cos_forward(n, e):
    half = n // 2
    if n % 4:
        return [weighted([(e[j], cosine(j, k, n)) for j in range(half + 1)]) for k in range(half + 1)]
    even = cos_forward(half, e[0::2])
    out = [None] * (half + 1)
    for k in range(n // 4 + 1):
        odd = weighted([(e[j], cosine(j, k, n)) for j in range(1, half, 2)])
        out[k] = plus(even[k], odd)
        if k < n // 4:
            out[half - k] = minus(even[k], odd)
    return out


def sin_forward(n, o):
    half = n // 2
    if n % 4:
        return [weighted([(o[j], sine(j, k, n)) for j in range(1, half)]) if k % half else None for k in range(half + 1)]
    even = sin_forward(half, o[0::2])
    out = [None] * (half + 1)
    for k in range(1, n // 4 + 1):
        odd = weighted([(o[j], sine(j, k, n)) for j in range(1, half, 2)])
        out[k] = plus(even[k], odd) if k < n // 4 else odd
        if k < n // 4:
            out[half - k] = minus(odd, even[k])
    return out


def cos_inverse(n, f, wanted):
    half, quarter = n // 2, n // 4
    if n % 4:
        return {x: weighted([(f[k], cosine(k, x, n)) for k in range(half + 1)]) for x in wanted}
    out = {}
    evens = [x // 2 for x in wanted if x % 2 == 0]
    odds = [x for x in wanted if x % 2]
    if odds:
        q = [minus(f[k], f[half - k]) for k in range(quarter)]
        for x in odds:
            out[x] = weighted([(q[k], cosine(k, x, n)) for k in range(quarter)])
    if evens:
        p = [plus(f[k], f[half - k]) for k in range(quarter)] + [f[quarter]]
        for x, value in cos_inverse(half, p, evens).items():
            out[2 * x] = value
    return out


def sin_inverse(n, g, wanted):
    half, quarter = n // 2, n // 4
    if n % 4:
        return {x: weighted([(g[k], sine(k, x, n)) for k in range(1, half)]) for x in wanted}
    out = {}
    evens = [x // 2 for x in wanted if x % 2 == 0]
    odds = [x for x in wanted if x % 2]
    if odds:
        t = [None] + [plus(g[k], g[half - k]) for k in range(1, quarter)] + [g[quarter]]
        for x in odds:
            out[x] = weighted([(t[k], sine(k, x, n)) for k in range(1, quarter + 1)])
    if evens:
        r = [None] + [minus(g[k], g[half - k]) for k in range(1, quarter)] + [None]
        for x, value in sin_inverse(half, r, evens).items():
            out[2 * x] = value
    return out


def slices_forward(s):
    e = [s[0]] + [plus(s[j], s[LENGTH - j]) for j in range(1, HALF)] + [s[HALF]]
    o = [None] + [minus(s[j], s[LENGTH - j]) for j in range(1, HALF)] + [None]
    return cos_forward(LENGTH, e), sin_forward(LENGTH, o)


def tables():
    def table(rows, cols):
        angle = (np.outer(np.arange(rows), np.arange(cols)) % WIDE).astype(np.float32)
        angle = angle * np.float32(2.0 * math.pi / WIDE)
        return np.cos(angle), np.sin(angle)

    c, s = table(WIDE, WIDE)
    first = np.block([[c, -s], [s, c]])
    second = np.block([[c, s], [-s, c]])
    small_z, small_y = [], []
    for flip in (False, True):
        c, s = table(EDGE, WIDE)
        if flip:
            c, s = c[::-1], s[::-1]
        small_z.append(np.block([[c, -s], [s, c]]))
        small_y.append(np.block([[c.T, s.T], [-s.T, c.T]]))
    behind = (np.arange(WIDE)[:, None] - np.arange(WIDE)[None, :]) % WIDE
    band = np.concatenate([behind < EDGE] * 3)
    return [
        jnp.asarray(t.astype(np.float32)).astype(BF16)
        for t in (first, second, np.stack(small_z), np.stack(small_y), band)
    ]


def dot(a, b):
    return jnp.dot(a, b, preferred_element_type=F32)


def spot(k):
    return k // 2, (k % 2) * WIDE


def fill_halo(core_ref, own_ref, other_ref, halo_ref):
    core = core_ref[0]
    for hop in range(2):
        halo_ref[pl.ds(hop * SLAB + 8 * core, 8)] = own_ref[hop]
        halo_ref[pl.ds(hop * SLAB + 8 * (1 - core), 8)] = other_ref[hop]


def load_rows(tomo_ref, halo_ref, at):
    s = [tomo_ref[j, at, :] if j < SLAB else halo_ref[j - SLAB, at, :] for j in range(LENGTH - 1)]
    return [value.astype(F32) for value in s]


def spectrum_kernel(core_ref, tomo_ref, own_ref, other_ref, first_ref, second_ref, spec_ref,
                    halo_ref, x_ref, z_ref):
    fill_halo(core_ref, own_ref, other_ref, halo_ref)

    def rows(step, carry):
        at = pl.ds(pl.multiple_of(step * 16, 16), 16)
        real, imag = slices_forward(load_rows(tomo_ref, halo_ref, at) + [None])
        for k in range(FREQS):
            x_ref[k, at, :WIDE] = real[k].astype(BF16)
            if imag[k] is None:
                x_ref[k, at, WIDE:] = jnp.zeros((16, WIDE), BF16)
            else:
                x_ref[k, at, WIDE:] = (-imag[k]).astype(BF16)
        return carry

    lax.fori_loop(0, WIDE // 16, rows, 0)

    for k in range(FREQS):
        pair, lane = spot(k)
        moved = dot(x_ref[k], first_ref[...]).astype(BF16)
        z_ref[pair, :WIDE, lane:lane + WIDE] = moved[:, :WIDE]
        z_ref[pair, WIDE:, lane:lane + WIDE] = moved[:, WIDE:]
    for pair in range(PAIRS):
        width = WIDE if pair == PAIRS - 1 else 2 * WIDE
        spec_ref[pair, :, :width] = dot(second_ref[...], z_ref[pair, :, :width]).astype(BF16)
        if width == WIDE:
            spec_ref[pair, :, WIDE:] = jnp.zeros((2 * WIDE, WIDE), BF16)


def split(value):
    high = value.astype(BF16)
    rest = value - high.astype(F32)
    middle = rest.astype(BF16)
    return high, middle, (rest - middle.astype(F32)).astype(BF16)


def factor_kernel(core_ref, tomo_ref, own_ref, other_ref, band_ref, factor_ref, halo_ref, sum_ref, square_ref):
    fill_halo(core_ref, own_ref, other_ref, halo_ref)

    def windows(step, carry):
        at = pl.ds(pl.multiple_of(step * 16, 16), 16)
        s = load_rows(tomo_ref, halo_ref, at)
        for target, field in ((sum_ref, s), (square_ref, [value * value for value in s])):
            for reach in (1, 2, 4, 8, 16):
                field = [field[j] + field[j + reach] for j in range(len(field) - reach)]
            for x in range(SLAB):
                target[x, at, :] = field[x]
        return carry

    lax.fori_loop(0, WIDE // 16, windows, 0)

    volume = float(EDGE**3)

    def along_y(field):
        for reach in (1, 2, 4, 8, 16):
            field = field + pltpu.roll(field, WIDE - reach, 0)
        return jnp.concatenate(split(field), axis=1)

    def scale(x, carry):
        both = jnp.concatenate([along_y(sum_ref[x]), along_y(square_ref[x])], axis=0)
        box = dot(both, band_ref[...]) / volume
        mean_t, mean_sq = box[:WIDE], box[WIDE:]
        root = lax.rsqrt(mean_sq - mean_t * mean_t + 1e-05) / jnp.float32(math.sqrt(volume))
        factor_ref[x] = root * jnp.float32(2.0 / (LENGTH * WIDE * WIDE))
        return carry

    lax.fori_loop(0, SLAB, scale, 0, unroll=4)


def spectrum_call(core, tomogram, own, other, first, second):
    vmem = pl.BlockSpec(memory_space=pltpu.VMEM)
    return pl.pallas_call(
        spectrum_kernel,
        out_shape=jax.ShapeDtypeStruct((PAIRS, 2 * WIDE, 2 * WIDE), BF16),
        in_specs=[pl.BlockSpec(memory_space=pltpu.SMEM)] + [vmem] * 5,
        out_specs=vmem,
        scratch_shapes=[
            pltpu.VMEM((2 * SLAB, WIDE, WIDE), BF16),
            pltpu.VMEM((FREQS, WIDE, 2 * WIDE), BF16),
            pltpu.VMEM((PAIRS, 2 * WIDE, 2 * WIDE), BF16),
        ],
        compiler_params=pltpu.CompilerParams(vmem_limit_bytes=40 << 20),
        cost_estimate=pl.CostEstimate(flops=4_000_000_000, transcendentals=0, bytes_accessed=6_000_000),
        name="spectrum",
    )(core, tomogram, own, other, first, second)


def factor_call(core, tomogram, own, other, band):
    vmem = pl.BlockSpec(memory_space=pltpu.VMEM)
    return pl.pallas_call(
        factor_kernel,
        out_shape=jax.ShapeDtypeStruct((SLAB, WIDE, WIDE), F32),
        in_specs=[pl.BlockSpec(memory_space=pltpu.SMEM)] + [vmem] * 4,
        out_specs=vmem,
        scratch_shapes=[
            pltpu.VMEM((2 * SLAB, WIDE, WIDE), BF16),
            pltpu.VMEM((SLAB, WIDE, WIDE), F32),
            pltpu.VMEM((SLAB, WIDE, WIDE), F32),
        ],
        compiler_params=pltpu.CompilerParams(vmem_limit_bytes=40 << 20),
        cost_estimate=pl.CostEstimate(flops=4_000_000_000, transcendentals=0, bytes_accessed=6_000_000),
        name="factor",
    )(core, tomogram, own, other, band)


def prep_kernel(core_ref, orient_ref, temp_ref, packed_ref):
    values = temp_ref[0].astype(F32).reshape(SLAB * EDGE, EDGE)
    rows = 4 * EDGE
    packed = jnp.concatenate([values[g * rows:(g + 1) * rows] for g in range(4)], axis=1).astype(BF16)
    index = jnp.full((TAIL, WIDE), orient_ref[0], jnp.int32).astype(F32).astype(BF16)
    for member in range(packed_ref.shape[0]):
        packed_ref[member, :WIDE] = packed
        packed_ref[member, WIDE:] = index


def prep_call(core, orient, templates, members):
    return pl.pallas_call(
        prep_kernel,
        out_shape=jax.ShapeDtypeStruct((members, WIDE + TAIL, WIDE), BF16),
        grid_spec=pltpu.PrefetchScalarGridSpec(
            num_scalar_prefetch=2,
            grid=(1,),
            in_specs=[
                pl.BlockSpec((1, EDGE // 2, EDGE, EDGE), lambda i, core, orient: (0, core[0], 0, 0)),
            ],
            out_specs=pl.BlockSpec((members, WIDE + TAIL, WIDE), lambda i, core, orient: (0, 0, 0)),
        ),
        name="prep",
    )(core, orient, templates)


def match_kernel(core_ref, orient_ref, across_ref, own_ref, other_ref, spec_ref, factor_ref, first_ref, second_ref,
                 small_z_ref, small_y_ref, best_ref,
                 base_ref, cube_ref, cube_out_ref, packed_ref, a_ref, z_ref, p_ref, q_ref, f_ref, held_ref):
    core = core_ref[0]
    for mine, half_ref in ((core, own_ref), (1 - core, other_ref)):
        values = half_ref[:WIDE].astype(F32)
        for group in range(4):
            start = pl.multiple_of((16 * mine + 4 * group) * EDGE, 128)
            base_ref[pl.ds(start, 4 * EDGE), :] = values[:, group * EDGE:(group + 1) * EDGE]
    values = base_ref[...]
    total = float(EDGE**3)
    center = jnp.sum(values) / total
    values = values - center
    spread = jnp.sum(values * values) / total
    base_ref[...] = (values * lax.rsqrt(spread + 1e-05)).astype(BF16).astype(F32)

    across = jnp.max(across_ref[WIDE:].astype(F32)).astype(jnp.int32)

    def orientation(step, carry):
        index = jnp.where(step == 0, orient_ref[0], across)
        order = index // 4
        flips = index % 4
        odd_order = order >= 3
        turn_a = (order == 2) | (order == 3) | (order == 4)
        turn_b = (order == 1) | (order == 2) | (order == 4) | (order == 5)
        turn_c = (order == 1) | (order == 4)
        flip_y = flips % 2
        flip_z = flips // 2
        middle = ((flips == 1) | (flips == 2)).astype(jnp.int32)
        flip_x = jnp.where(odd_order, 1 - middle, middle)

        def swap_last(source, target):
            for a in range(EDGE):
                at = slice(a * EDGE, (a + 1) * EDGE)
                target[at, :] = source[at, :].T

        def copy(source, target):
            target[...] = source[...]

        @pl.when(turn_a)
        def _():
            swap_last(base_ref, cube_ref)

        @pl.when(jnp.logical_not(turn_a))
        def _():
            copy(base_ref, cube_ref)

        @pl.when(turn_b)
        def _():
            for b in range(EDGE):
                cube_out_ref[b * EDGE:(b + 1) * EDGE, :] = cube_ref[pl.ds(b, EDGE, stride=EDGE), :]

        @pl.when(jnp.logical_not(turn_b))
        def _():
            copy(cube_ref, cube_out_ref)

        @pl.when(turn_c)
        def _():
            swap_last(cube_out_ref, cube_ref)

        @pl.when(jnp.logical_not(turn_c))
        def _():
            copy(cube_out_ref, cube_ref)

        for x in range(EDGE):
            tile = cube_ref[x * EDGE:(x + 1) * EDGE, :]
            packed_ref[x] = jnp.concatenate([tile[8 * g:8 * g + 8] for g in range(4)], axis=1)

        s = [None] * LENGTH
        for i in range(EDGE):
            s[i + SLAB // 2] = packed_ref[jnp.where(flip_x == 1, EDGE - 1 - i, i)]
        real, imag = slices_forward(s)
        for k in range(FREQS):
            share = 0.5 if k in (0, HALF) else 1.0
            for g in range(4):
                at = slice(k * EDGE + 8 * g, k * EDGE + 8 * g + 8)
                lanes = slice(g * EDGE, (g + 1) * EDGE)
                a_ref[at, :EDGE] = real[k][:, lanes] * jnp.float32(share)
                if imag[k] is None:
                    a_ref[at, EDGE:2 * EDGE] = jnp.zeros((8, EDGE), F32)
                else:
                    a_ref[at, EDGE:2 * EDGE] = -imag[k][:, lanes]

        moved = dot(a_ref[...].astype(BF16), small_z_ref[flip_z]).astype(BF16)
        for k in range(FREQS):
            pair, lane = spot(k)
            part = moved[k * EDGE:(k + 1) * EDGE]
            z_ref[pair, :EDGE, lane:lane + WIDE] = part[:, :WIDE]
            z_ref[pair, EDGE:, lane:lane + WIDE] = part[:, WIDE:]

        small_y = small_y_ref[flip_y]
        for pair in range(PAIRS):
            width = WIDE if pair == PAIRS - 1 else 2 * WIDE
            temp = dot(small_y, z_ref[pair, :, :width])
            slab = spec_ref[pair, :, :width].astype(F32)
            temp_r, temp_i = temp[:WIDE], temp[WIDE:]
            slab_r, slab_i = slab[:WIDE], slab[WIDE:]
            prod_r = (slab_r * temp_r + slab_i * temp_i).astype(BF16)
            prod_i = (slab_i * temp_r - slab_r * temp_i).astype(BF16)
            for part in range(width // WIDE):
                k = 2 * pair + part
                lanes = slice(part * WIDE, (part + 1) * WIDE)
                p_ref[k, :, :WIDE] = prod_r[:, lanes]
                p_ref[k, :, WIDE:] = prod_i[:, lanes]

        for k in range(FREQS):
            pair, lane = spot(k)
            moved = dot(p_ref[k], second_ref[...]).astype(BF16)
            q_ref[pair, :WIDE, lane:lane + WIDE] = moved[:, :WIDE]
            q_ref[pair, WIDE:, lane:lane + WIDE] = moved[:, WIDE:]
        for pair in range(PAIRS):
            width = WIDE if pair == PAIRS - 1 else 2 * WIDE
            f_ref[pair, :, :width] = dot(first_ref[...], q_ref[pair, :, :width])

        def scores(block, finish):
            at = pl.multiple_of(block * 8, 8)
            fr, fi = [], []
            for k in range(FREQS):
                pair, lane = spot(k)
                fr.append(f_ref[pair, pl.ds(at, 8), lane:lane + WIDE])
                fi.append(f_ref[pair, pl.ds(WIDE + at, 8), lane:lane + WIDE])
            reach = SLAB // 2
            even = cos_inverse(LENGTH, fr, list(range(reach + 1)))
            odd = sin_inverse(LENGTH, fi, list(range(1, reach + 1)))
            for x in range(SLAB):
                lag = x - reach
                if lag == 0:
                    value = even[0]
                elif lag > 0:
                    value = even[lag] - odd[lag]
                else:
                    value = even[-lag] + odd[-lag]
                finish(x, pl.ds(at, 8), value * factor_ref[x, pl.ds(at, 8), :])

        @pl.when(step == 0)
        def _():
            def body(block, carry):
                def keep(x, at, value):
                    held_ref[x, at, :] = value

                scores(block, keep)
                return carry

            lax.fori_loop(0, WIDE // 8, body, 0)

        @pl.when(step == 1)
        def _():
            def body(block, carry):
                def keep(x, at, value):
                    held_ref[x, at, :] = jnp.maximum(held_ref[x, at, :], value)

                scores(block, keep)
                return carry

            lax.fori_loop(0, WIDE // 8, body, 0)

        return carry

    lax.fori_loop(0, 2, orientation, 0)
    best_ref[...] = held_ref[...].astype(BF16)


def match_call(core, orient, across, own, other, spec, factor, first, second, small_z, small_y):
    vmem = pl.BlockSpec(memory_space=pltpu.VMEM)
    smem = pl.BlockSpec(memory_space=pltpu.SMEM)
    cube = EDGE * EDGE
    return pl.pallas_call(
        match_kernel,
        out_shape=jax.ShapeDtypeStruct((SLAB, WIDE, WIDE), BF16),
        in_specs=[smem, smem] + [vmem] * 9,
        out_specs=vmem,
        scratch_shapes=[
            pltpu.VMEM((cube, EDGE), F32),
            pltpu.VMEM((cube, EDGE), F32),
            pltpu.VMEM((cube, EDGE), F32),
            pltpu.VMEM((EDGE, 8, WIDE), F32),
            pltpu.VMEM((FREQS * EDGE, 2 * EDGE), F32),
            pltpu.VMEM((PAIRS, 2 * EDGE, 2 * WIDE), BF16),
            pltpu.VMEM((FREQS, WIDE, 2 * WIDE), BF16),
            pltpu.VMEM((PAIRS, 2 * WIDE, 2 * WIDE), BF16),
            pltpu.VMEM((PAIRS, 2 * WIDE, 2 * WIDE), F32),
            pltpu.VMEM((SLAB, WIDE, WIDE), F32),
        ],
        compiler_params=pltpu.CompilerParams(vmem_limit_bytes=40 << 20),
        cost_estimate=pl.CostEstimate(flops=8_000_000_000, transcendentals=0, bytes_accessed=6_000_000),
        name="match",
    )(core, orient, across, own, other, spec, factor, first, second, small_z, small_y)


def shifted(value, axis, by):
    length = lax.axis_size(axis)
    pairs = [(i, i + by) for i in range(length) if 0 <= i + by < length]
    return lax.ppermute(value, axis, pairs)


def swapped(value, axis):
    return lax.ppermute(value, axis, [(0, 1), (1, 0)])


def by_offset(value, axes, offset):
    sizes = [lax.axis_size(axis) for axis in axes]

    def flat(spots):
        index = 0
        for spot_at, size in zip(spots, sizes):
            index = index * size + spot_at % size
        return index

    pairs = [
        (flat(spots), flat([at + by for at, by in zip(spots, offset)]))
        for spots in itertools.product(*[range(size) for size in sizes])
    ]
    return lax.ppermute(value, axes, pairs)


def shards(tomogram, templates, owners, orient_ids, slice_mask):
    core_arg = lax.axis_index("core").astype(jnp.int32)[None]
    first, second, small_z, small_y, band = tables()
    rows, columns = lax.axis_size("tile_1"), lax.axis_size("tile_2")
    members = lax.axis_size("tile_0")
    root_x = lax.rem(owners[0], columns)
    root_y = lax.rem(lax.div(owners[0], columns), rows)
    root_z = lax.div(owners[0], rows * columns)
    off_y = lax.rem(lax.axis_index("tile_1") + rows - root_y, rows)
    off_x = lax.rem(lax.axis_index("tile_2") + columns - root_x, columns)
    even_y = lax.rem(off_y, 2) == 0

    sent = prep_call(core_arg, orient_ids[0], templates, members)
    got = lax.all_to_all(sent, "tile_0", 0, 0, tiled=True)
    half = lax.dynamic_index_in_dim(got, root_z, 0, keepdims=False)

    slices = lax.dynamic_slice_in_dim(tomogram, SLAB // 2 * lax.axis_index("core"), SLAB // 2, 0)
    near = shifted(slices, TILE, -1)
    far = shifted(slices, TILE, -2)
    halo = jnp.stack([near, far])
    other_halo = swapped(halo, "core")

    axes = ("tile_1", "tile_2", "far")
    half = jnp.where(off_y == 2, by_offset(half, axes, (2, 0, 0)), half)
    from_y = by_offset(half, axes, (1, 0, 0))
    from_x = by_offset(half, axes, (0, 1, 1))
    from_both = by_offset(half, axes, (1, 1, 1))
    half = jnp.where(
        off_x == 0, jnp.where(even_y, half, from_y), jnp.where(even_y, from_x, from_both)
    )
    other_half = swapped(half, "core")

    factor = factor_call(core_arg, tomogram, halo, other_halo, band)
    spec = spectrum_call(core_arg, tomogram, halo, other_halo, first, second)

    best = match_call(core_arg, orient_ids[0], from_x, half, other_half, spec, factor, first, second, small_z, small_y)
    best = jnp.maximum(best, swapped(best, "core"))
    return best.astype(F32) * slice_mask.astype(F32)[:, None, None]


def solution(mesh):
    torus = Mesh(
        mesh.devices.reshape(8, 4, 2, 2, 2), ("tile_0", "tile_1", "tile_2", "far", "core")
    )
    in_specs = (P(TILE, None, None), P(TILE, None, None, None), P(), P(None, ("far", "core")), P(TILE))
    out_specs = P(TILE, None, None)
    return jax.shard_map(
        shards, mesh=torus, in_specs=in_specs, out_specs=out_specs, check_vma=False
    )
```

```python
import math

import jax
import jax.numpy as jnp
import numpy as np
from jax import lax
from jax.experimental import pallas as pl
from jax.experimental.pallas import tpu as pltpu
from jax.sharding import Mesh
from jax.sharding import PartitionSpec as P


TILE = ("tile_0", "tile_1", "tile_2")
EDGE = 32
SLAB = 16
WIDE = 128
LENGTH = 48
HALF = LENGTH // 2
FREQS = HALF + 1
PAIRS = (FREQS + 1) // 2
BF16 = jnp.bfloat16
F32 = jnp.float32


def plus(a, b):
    if a is None:
        return b
    return a if b is None else a + b


def minus(a, b):
    if b is None:
        return a
    return -b if a is None else a - b


def weighted(terms):
    total = None
    for value, weight in terms:
        if value is None or abs(weight) < 1e-9:
            continue
        if abs(abs(weight) - 1.0) < 1e-9:
            part = value
        else:
            part = value * jnp.float32(abs(weight))
        if weight > 0:
            total = plus(total, part)
        else:
            total = minus(total, part)
    return total


def cosine(j, k, n):
    return math.cos(2.0 * math.pi * ((j * k) % n) / n)


def sine(j, k, n):
    return math.sin(2.0 * math.pi * ((j * k) % n) / n)


def cos_forward(n, e):
    half = n // 2
    if n % 4:
        return [weighted([(e[j], cosine(j, k, n)) for j in range(half + 1)]) for k in range(half + 1)]
    even = cos_forward(half, e[0::2])
    out = [None] * (half + 1)
    for k in range(n // 4 + 1):
        odd = weighted([(e[j], cosine(j, k, n)) for j in range(1, half, 2)])
        out[k] = plus(even[k], odd)
        if k < n // 4:
            out[half - k] = minus(even[k], odd)
    return out


def sin_forward(n, o):
    half = n // 2
    if n % 4:
        return [weighted([(o[j], sine(j, k, n)) for j in range(1, half)]) if k % half else None for k in range(half + 1)]
    even = sin_forward(half, o[0::2])
    out = [None] * (half + 1)
    for k in range(1, n // 4 + 1):
        odd = weighted([(o[j], sine(j, k, n)) for j in range(1, half, 2)])
        out[k] = plus(even[k], odd) if k < n // 4 else odd
        if k < n // 4:
            out[half - k] = minus(odd, even[k])
    return out


def cos_inverse(n, f, wanted):
    half, quarter = n // 2, n // 4
    if n % 4:
        return {x: weighted([(f[k], cosine(k, x, n)) for k in range(half + 1)]) for x in wanted}
    out = {}
    evens = [x // 2 for x in wanted if x % 2 == 0]
    odds = [x for x in wanted if x % 2]
    if odds:
        q = [minus(f[k], f[half - k]) for k in range(quarter)]
        for x in odds:
            out[x] = weighted([(q[k], cosine(k, x, n)) for k in range(quarter)])
    if evens:
        p = [plus(f[k], f[half - k]) for k in range(quarter)] + [f[quarter]]
        for x, value in cos_inverse(half, p, evens).items():
            out[2 * x] = value
    return out


def sin_inverse(n, g, wanted):
    half, quarter = n // 2, n // 4
    if n % 4:
        return {x: weighted([(g[k], sine(k, x, n)) for k in range(1, half)]) for x in wanted}
    out = {}
    evens = [x // 2 for x in wanted if x % 2 == 0]
    odds = [x for x in wanted if x % 2]
    if odds:
        t = [None] + [plus(g[k], g[half - k]) for k in range(1, quarter)] + [g[quarter]]
        for x in odds:
            out[x] = weighted([(t[k], sine(k, x, n)) for k in range(1, quarter + 1)])
    if evens:
        r = [None] + [minus(g[k], g[half - k]) for k in range(1, quarter)] + [None]
        for x, value in sin_inverse(half, r, evens).items():
            out[2 * x] = value
    return out


def slices_forward(s):
    e = [s[0]] + [plus(s[j], s[LENGTH - j]) for j in range(1, HALF)] + [s[HALF]]
    o = [None] + [minus(s[j], s[LENGTH - j]) for j in range(1, HALF)] + [None]
    return cos_forward(LENGTH, e), sin_forward(LENGTH, o)


def tables():
    def table(rows, cols):
        angle = (np.outer(np.arange(rows), np.arange(cols)) % WIDE).astype(np.float32)
        angle = angle * np.float32(2.0 * math.pi / WIDE)
        return np.cos(angle), np.sin(angle)

    c, s = table(WIDE, WIDE)
    first = np.block([[c, -s], [s, c]])
    second = np.block([[c, s], [-s, c]])
    small_z, small_y = [], []
    for flip in (False, True):
        c, s = table(EDGE, WIDE)
        if flip:
            c, s = c[::-1], s[::-1]
        small_z.append(np.block([[c, -s], [s, c]]))
        small_y.append(np.block([[c.T, s.T], [-s.T, c.T]]))
    return [
        jnp.asarray(t.astype(np.float32)).astype(BF16)
        for t in (first, second, np.stack(small_z), np.stack(small_y))
    ]


def dot(a, b):
    return jnp.dot(a, b, preferred_element_type=F32)


def spot(k):
    return k // 2, (k % 2) * WIDE


def split(value):
    high = value.astype(BF16)
    rest = value - high.astype(F32)
    middle = rest.astype(BF16)
    return high, middle, (rest - middle.astype(F32)).astype(BF16)


def load_rows(tomo_ref, near_ref, far_ref, at):
    s = []
    for ref, count in ((tomo_ref, SLAB), (near_ref, SLAB), (far_ref, SLAB - 1)):
        s += [ref[j, at, :].astype(F32) for j in range(count)]
    return s


def slab_kernel(core_ref, tomo_hbm, own_ref, other_ref, first_ref, second_ref, spec_ref, factor_ref,
                tomo_ref, x_ref, z_ref, sum_ref, square_ref, tomo_sem):
    core = core_ref[0]
    fetch = pltpu.make_async_copy(tomo_hbm, tomo_ref, tomo_sem)
    fetch.start()
    fetch.wait()

    def along_x(near_ref, far_ref):
        def rows(step, carry):
            at = pl.ds(pl.multiple_of(step * 16, 16), 16)
            real, imag = slices_forward(load_rows(tomo_ref, near_ref, far_ref, at) + [None])
            for k in range(FREQS):
                x_ref[k, at, :WIDE] = real[k].astype(BF16)
                if imag[k] is None:
                    x_ref[k, at, WIDE:] = jnp.zeros((16, WIDE), BF16)
                else:
                    x_ref[k, at, WIDE:] = (-imag[k]).astype(BF16)
            return carry

        def windows(step, carry):
            at = pl.ds(pl.multiple_of(step * 16, 16), 16)
            s = load_rows(tomo_ref, near_ref, far_ref, at)
            for target, field in ((sum_ref, s), (square_ref, [value * value for value in s])):
                for reach in (1, 2, 4, 8, 16):
                    field = [field[j] + field[j + reach] for j in range(len(field) - reach)]
                for x in range(SLAB):
                    target[x, at, :] = field[x]
            return carry

        lax.fori_loop(0, WIDE // 16, rows, 0)
        lax.fori_loop(0, WIDE // 16, windows, 0)

    @pl.when(core == 0)
    def _():
        along_x(own_ref, other_ref)

    @pl.when(core != 0)
    def _():
        along_x(other_ref, own_ref)

    for k in range(FREQS):
        pair, lane = spot(k)
        moved = dot(x_ref[k], first_ref[...]).astype(BF16)
        z_ref[pair, :WIDE, lane:lane + WIDE] = moved[:, :WIDE]
        z_ref[pair, WIDE:, lane:lane + WIDE] = moved[:, WIDE:]
    for pair in range(PAIRS):
        width = WIDE if pair == PAIRS - 1 else 2 * WIDE
        spec_ref[pair, :, :width] = dot(second_ref[...], z_ref[pair, :, :width]).astype(BF16)
        if width == WIDE:
            spec_ref[pair, :, WIDE:] = jnp.zeros((2 * WIDE, WIDE), BF16)

    volume = float(EDGE**3)
    ahead = lax.broadcasted_iota(jnp.int32, (WIDE, WIDE), 0) - lax.broadcasted_iota(jnp.int32, (WIDE, WIDE), 1)
    band = (jnp.where(ahead < 0, ahead + WIDE, ahead) < EDGE).astype(F32).astype(BF16)
    band = jnp.concatenate([band] * 3, axis=0)

    def along_y(field):
        for reach in (1, 2, 4, 8, 16):
            field = field + pltpu.roll(field, WIDE - reach, 0)
        return jnp.concatenate(split(field), axis=1)

    def scale(x, carry):
        both = jnp.concatenate([along_y(sum_ref[x]), along_y(square_ref[x])], axis=0)
        box = dot(both, band) / volume
        mean_t, mean_sq = box[:WIDE], box[WIDE:]
        root = lax.rsqrt(mean_sq - mean_t * mean_t + 1e-05) / jnp.float32(math.sqrt(volume))
        factor_ref[x] = root * jnp.float32(2.0 / (LENGTH * WIDE * WIDE))
        return carry

    lax.fori_loop(0, SLAB, scale, 0, unroll=4)


def slab_call(core, tomogram, own, other, first, second):
    vmem = pl.BlockSpec(memory_space=pltpu.VMEM)
    return pl.pallas_call(
        slab_kernel,
        out_shape=(
            jax.ShapeDtypeStruct((PAIRS, 2 * WIDE, 2 * WIDE), BF16),
            jax.ShapeDtypeStruct((SLAB, WIDE, WIDE), F32),
        ),
        in_specs=[pl.BlockSpec(memory_space=pltpu.SMEM), pl.BlockSpec(memory_space=pl.ANY)] + [vmem] * 4,
        out_specs=(vmem, vmem),
        scratch_shapes=[
            pltpu.VMEM((SLAB, WIDE, WIDE), BF16),
            pltpu.VMEM((FREQS, WIDE, 2 * WIDE), BF16),
            pltpu.VMEM((PAIRS, 2 * WIDE, 2 * WIDE), BF16),
            pltpu.VMEM((SLAB, WIDE, WIDE), F32),
            pltpu.VMEM((SLAB, WIDE, WIDE), F32),
            pltpu.SemaphoreType.DMA,
        ],
        compiler_params=pltpu.CompilerParams(vmem_limit_bytes=40 << 20),
        cost_estimate=pl.CostEstimate(flops=4_000_000_000, transcendentals=0, bytes_accessed=6_000_000),
        name="slab",
    )(core, tomogram, own, other, first, second)


def prep_kernel(core_ref, temp_ref, packed_ref):
    values = temp_ref[0].astype(F32).reshape(SLAB * EDGE, EDGE)
    rows = 4 * EDGE
    packed = jnp.concatenate([values[g * rows:(g + 1) * rows] for g in range(4)], axis=1).astype(BF16)
    for member in range(packed_ref.shape[0]):
        packed_ref[member] = packed


def prep_call(core, templates, members):
    return pl.pallas_call(
        prep_kernel,
        out_shape=jax.ShapeDtypeStruct((members, WIDE, WIDE), BF16),
        grid_spec=pltpu.PrefetchScalarGridSpec(
            num_scalar_prefetch=1,
            grid=(1,),
            in_specs=[
                pl.BlockSpec((1, EDGE // 2, EDGE, EDGE), lambda i, core: (0, core[0], 0, 0)),
            ],
            out_specs=pl.BlockSpec((members, WIDE, WIDE), lambda i, core: (0, 0, 0)),
        ),
        name="prep",
    )(core, templates)


def turns_of(index):
    order, flips = lax.div(index, 4), lax.rem(index, 4)
    turn_a = (order == 2) | (order == 3) | (order == 4)
    turn_b = (order == 1) | (order == 2) | (order == 4) | (order == 5)
    turn_c = (order == 1) | (order == 4)
    middle = ((flips == 1) | (flips == 2)).astype(jnp.int32)
    flip_x = jnp.where(order >= 3, 1 - middle, middle)
    return (turn_a, turn_b, turn_c), (flip_x, lax.rem(flips, 2), lax.div(flips, 2))


def swap_last(source, target):
    for a in range(EDGE):
        at = slice(a * EDGE, (a + 1) * EDGE)
        target[at, :] = source[at, :].T


def swap_first(source, target):
    for b in range(EDGE):
        target[b * EDGE:(b + 1) * EDGE, :] = source[pl.ds(b, EDGE, stride=EDGE), :]


def turn(base_ref, cube_ref, spare_ref, turns):
    source = base_ref
    for asked, swap, target in zip(turns, (swap_last, swap_first, swap_last), (cube_ref, spare_ref, cube_ref)):
        def moved(swap=swap, source=source, target=target):
            swap(source, target)

        def kept(source=source, target=target):
            target[...] = source[...]

        pl.when(asked)(moved)
        pl.when(jnp.logical_not(asked))(kept)
        source = target


def match_kernel(core_ref, orient_ref, across_ref, own_ref, other_ref, spec_ref, factor_ref, first_ref, second_ref,
                 small_z_ref, small_y_ref, best_ref,
                 base_ref, cube_ref, spare_ref, packed_ref, a_ref, z_ref, p_ref, q_ref, f_ref):
    core = core_ref[0]
    halves = [ref[...].astype(F32) for ref in (own_ref, other_ref)]
    total = float(EDGE**3)
    center = jnp.sum(halves[0] + halves[1]) / total
    halves = [half - center for half in halves]
    spread = jnp.sum(halves[0] * halves[0] + halves[1] * halves[1]) / total
    root = lax.rsqrt(spread + 1e-05)
    for mine, half in zip((core, 1 - core), halves):
        half = (half * root).astype(BF16).astype(F32)
        for group in range(4):
            start = pl.multiple_of((16 * mine + 4 * group) * EDGE, 128)
            base_ref[pl.ds(start, 4 * EDGE), :] = half[:, group * EDGE:(group + 1) * EDGE]

    flips = []
    for o, index in enumerate((orient_ref[0], across_ref[0])):
        turns, flipped = turns_of(index)
        flips.append(flipped)
        turn(base_ref, cube_ref.at[o], spare_ref.at[o], turns)

    for o in range(2):
        for x in range(EDGE):
            tile = cube_ref[o, x * EDGE:(x + 1) * EDGE, :]
            packed_ref[o, x] = jnp.concatenate([tile[8 * g:8 * g + 8] for g in range(4)], axis=1)

    for o in range(2):
        s = [None] * LENGTH
        for i in range(EDGE):
            s[i + SLAB // 2] = packed_ref[o, jnp.where(flips[o][0] == 1, EDGE - 1 - i, i)]
        real, imag = slices_forward(s)
        for k in range(FREQS):
            share = 0.5 if k in (0, HALF) else 1.0
            for g in range(4):
                at = slice(k * EDGE + 8 * g, k * EDGE + 8 * g + 8)
                lanes = slice(g * EDGE, (g + 1) * EDGE)
                a_ref[o, at, :EDGE] = real[k][:, lanes] * jnp.float32(share)
                if imag[k] is None:
                    a_ref[o, at, EDGE:2 * EDGE] = jnp.zeros((8, EDGE), F32)
                else:
                    a_ref[o, at, EDGE:2 * EDGE] = -imag[k][:, lanes]

    for o in range(2):
        moved = dot(a_ref[o].astype(BF16), small_z_ref[flips[o][2]]).astype(BF16)
        for k in range(FREQS):
            pair, lane = spot(k)
            part = moved[k * EDGE:(k + 1) * EDGE]
            z_ref[o, pair, :EDGE, lane:lane + WIDE] = part[:, :WIDE]
            z_ref[o, pair, EDGE:, lane:lane + WIDE] = part[:, WIDE:]

    for pair in range(PAIRS):
        width = WIDE if pair == PAIRS - 1 else 2 * WIDE
        slab = spec_ref[pair, :, :width].astype(F32)
        slab_r, slab_i = slab[:WIDE], slab[WIDE:]
        for o in range(2):
            temp = dot(small_y_ref[flips[o][1]], z_ref[o, pair, :, :width])
            temp_r, temp_i = temp[:WIDE], temp[WIDE:]
            prod_r = (slab_r * temp_r + slab_i * temp_i).astype(BF16)
            prod_i = (slab_i * temp_r - slab_r * temp_i).astype(BF16)
            for part in range(width // WIDE):
                k = 2 * pair + part
                lanes = slice(part * WIDE, (part + 1) * WIDE)
                p_ref[o, k, :, :WIDE] = prod_r[:, lanes]
                p_ref[o, k, :, WIDE:] = prod_i[:, lanes]

    for o in range(2):
        for k in range(FREQS):
            pair, lane = spot(k)
            moved = dot(p_ref[o, k], second_ref[...]).astype(BF16)
            q_ref[o, pair, :WIDE, lane:lane + WIDE] = moved[:, :WIDE]
            q_ref[o, pair, WIDE:, lane:lane + WIDE] = moved[:, WIDE:]
    for o in range(2):
        for pair in range(PAIRS):
            width = WIDE if pair == PAIRS - 1 else 2 * WIDE
            f_ref[o, pair, :, :width] = dot(first_ref[...], q_ref[o, pair, :, :width])

    def correlation(o, at):
        fr, fi = [], []
        for k in range(FREQS):
            pair, lane = spot(k)
            fr.append(f_ref[o, pair, pl.ds(at, 8), lane:lane + WIDE])
            fi.append(f_ref[o, pair, pl.ds(WIDE + at, 8), lane:lane + WIDE])
        reach = SLAB // 2
        even = cos_inverse(LENGTH, fr, list(range(reach + 1)))
        odd = sin_inverse(LENGTH, fi, list(range(1, reach + 1)))
        values = []
        for lag in range(-reach, SLAB - reach):
            if lag == 0:
                values.append(even[0])
            elif lag > 0:
                values.append(even[lag] - odd[lag])
            else:
                values.append(even[-lag] + odd[-lag])
        return values

    def scores(block, carry):
        at = pl.multiple_of(block * 16, 16)
        rows = []
        for part in (0, 8):
            pair = [correlation(o, at + part) for o in range(2)]
            rows.append([jnp.maximum(one, two) for one, two in zip(*pair)])
        for x in range(SLAB):
            value = jnp.concatenate([rows[0][x], rows[1][x]], axis=0) * factor_ref[x, pl.ds(at, 16), :]
            best_ref[x, pl.ds(at, 16), :] = value.astype(BF16)
        return carry

    lax.fori_loop(0, WIDE // 16, scores, 0)


def match_call(core, orient, across, own, other, spec, factor, first, second, small_z, small_y):
    vmem = pl.BlockSpec(memory_space=pltpu.VMEM)
    smem = pl.BlockSpec(memory_space=pltpu.SMEM)
    cube = EDGE * EDGE
    return pl.pallas_call(
        match_kernel,
        out_shape=jax.ShapeDtypeStruct((SLAB, WIDE, WIDE), BF16),
        in_specs=[smem] * 3 + [vmem] * 8,
        out_specs=vmem,
        scratch_shapes=[
            pltpu.VMEM((cube, EDGE), F32),
            pltpu.VMEM((2, cube, EDGE), F32),
            pltpu.VMEM((2, cube, EDGE), F32),
            pltpu.VMEM((2, EDGE, 8, WIDE), F32),
            pltpu.VMEM((2, FREQS * EDGE, 2 * EDGE), F32),
            pltpu.VMEM((2, PAIRS, 2 * EDGE, 2 * WIDE), BF16),
            pltpu.VMEM((2, FREQS, WIDE, 2 * WIDE), BF16),
            pltpu.VMEM((2, PAIRS, 2 * WIDE, 2 * WIDE), BF16),
            pltpu.VMEM((2, PAIRS, 2 * WIDE, 2 * WIDE), F32),
        ],
        compiler_params=pltpu.CompilerParams(vmem_limit_bytes=40 << 20),
        cost_estimate=pl.CostEstimate(flops=8_000_000_000, transcendentals=0, bytes_accessed=6_000_000),
        name="match",
    )(core, orient, across, own, other, spec, factor, first, second, small_z, small_y)


def swapped(value, axis):
    return lax.ppermute(value, axis, [(0, 1), (1, 0)])


def from_member(value, axis, root):
    sent = jnp.broadcast_to(value[None], (lax.axis_size(axis), *value.shape))
    got = lax.all_to_all(sent, axis, 0, 0, tiled=True)
    return lax.dynamic_index_in_dim(got, root, 0, keepdims=False)


def halo_pairs(tiles):
    return [
        (2 * tile + core, 2 * (tile - 1 - core) + core)
        for tile in range(tiles)
        for core in range(2)
        if tile - 1 - core >= 0
    ]


def shards(tomogram, templates, owners, orient_ids, slice_mask):
    core_arg = lax.axis_index("core").astype(jnp.int32)[None]
    first, second, small_z, small_y = tables()
    columns = lax.axis_size("tile_2")
    depth, plane = lax.axis_size("tile_0"), lax.axis_size("tile_1") * columns
    root_plane, root_z = lax.rem(owners[0], plane), lax.div(owners[0], plane)

    sent = prep_call(core_arg, templates, plane)
    got = lax.all_to_all(sent, ("tile_1", "tile_2"), 0, 0, tiled=True)
    half = lax.dynamic_index_in_dim(got, root_plane, 0, keepdims=False)

    halo = lax.ppermute(tomogram, TILE + ("core",), halo_pairs(depth * plane))
    across = swapped(orient_ids[0], "far")
    other_halo = swapped(halo, "core")

    half = from_member(half, "tile_0", root_z)
    other_half = swapped(half, "core")

    spec, factor = slab_call(core_arg, tomogram, halo, other_halo, first, second)

    best = match_call(core_arg, orient_ids[0], across, half, other_half, spec, factor, first, second, small_z, small_y)
    best = jnp.maximum(best, swapped(best, "core"))
    return best.astype(F32) * slice_mask.astype(F32)[:, None, None]


def solution(mesh):
    torus = Mesh(
        mesh.devices.reshape(8, 4, 2, 2, 2), ("tile_0", "tile_1", "tile_2", "far", "core")
    )
    in_specs = (P(TILE, None, None), P(TILE, None, None, None), P(), P(None, ("far", "core")), P(TILE))
    out_specs = P(TILE, None, None)
    return jax.shard_map(
        shards, mesh=torus, in_specs=in_specs, out_specs=out_specs, check_vma=False
    )
```

```python
import math

import jax
import jax.numpy as jnp
import numpy as np
from jax import lax
from jax.experimental import pallas as pl
from jax.experimental.pallas import tpu as pltpu
from jax.sharding import Mesh
from jax.sharding import PartitionSpec as P


TILE = ("tile_0", "tile_1", "tile_2")
EDGE = 32
SLAB = 16
WIDE = 128
LENGTH = 48
HALF = LENGTH // 2
FREQS = HALF + 1
PAIRS = (FREQS + 1) // 2
BF16 = jnp.bfloat16
F32 = jnp.float32


def plus(a, b):
    if a is None:
        return b
    return a if b is None else a + b


def minus(a, b):
    if b is None:
        return a
    return -b if a is None else a - b


def weighted(terms):
    total = None
    for value, weight in terms:
        if value is None or abs(weight) < 1e-9:
            continue
        if abs(abs(weight) - 1.0) < 1e-9:
            part = value
        else:
            part = value * jnp.float32(abs(weight))
        if weight > 0:
            total = plus(total, part)
        else:
            total = minus(total, part)
    return total


def cosine(j, k, n):
    return math.cos(2.0 * math.pi * ((j * k) % n) / n)


def sine(j, k, n):
    return math.sin(2.0 * math.pi * ((j * k) % n) / n)


def cos_forward(n, e):
    half = n // 2
    if n % 4:
        return [weighted([(e[j], cosine(j, k, n)) for j in range(half + 1)]) for k in range(half + 1)]
    even = cos_forward(half, e[0::2])
    out = [None] * (half + 1)
    for k in range(n // 4 + 1):
        odd = weighted([(e[j], cosine(j, k, n)) for j in range(1, half, 2)])
        out[k] = plus(even[k], odd)
        if k < n // 4:
            out[half - k] = minus(even[k], odd)
    return out


def sin_forward(n, o):
    half = n // 2
    if n % 4:
        return [weighted([(o[j], sine(j, k, n)) for j in range(1, half)]) if k % half else None for k in range(half + 1)]
    even = sin_forward(half, o[0::2])
    out = [None] * (half + 1)
    for k in range(1, n // 4 + 1):
        odd = weighted([(o[j], sine(j, k, n)) for j in range(1, half, 2)])
        out[k] = plus(even[k], odd) if k < n // 4 else odd
        if k < n // 4:
            out[half - k] = minus(odd, even[k])
    return out


def cos_inverse(n, f, wanted):
    half, quarter = n // 2, n // 4
    if n % 4:
        return {x: weighted([(f[k], cosine(k, x, n)) for k in range(half + 1)]) for x in wanted}
    out = {}
    evens = [x // 2 for x in wanted if x % 2 == 0]
    odds = [x for x in wanted if x % 2]
    if odds:
        q = [minus(f[k], f[half - k]) for k in range(quarter)]
        for x in odds:
            out[x] = weighted([(q[k], cosine(k, x, n)) for k in range(quarter)])
    if evens:
        p = [plus(f[k], f[half - k]) for k in range(quarter)] + [f[quarter]]
        for x, value in cos_inverse(half, p, evens).items():
            out[2 * x] = value
    return out


def sin_inverse(n, g, wanted):
    half, quarter = n // 2, n // 4
    if n % 4:
        return {x: weighted([(g[k], sine(k, x, n)) for k in range(1, half)]) for x in wanted}
    out = {}
    evens = [x // 2 for x in wanted if x % 2 == 0]
    odds = [x for x in wanted if x % 2]
    if odds:
        t = [None] + [plus(g[k], g[half - k]) for k in range(1, quarter)] + [g[quarter]]
        for x in odds:
            out[x] = weighted([(t[k], sine(k, x, n)) for k in range(1, quarter + 1)])
    if evens:
        r = [None] + [minus(g[k], g[half - k]) for k in range(1, quarter)] + [None]
        for x, value in sin_inverse(half, r, evens).items():
            out[2 * x] = value
    return out


def slices_forward(s):
    e = [s[0]] + [plus(s[j], s[LENGTH - j]) for j in range(1, HALF)] + [s[HALF]]
    o = [None] + [minus(s[j], s[LENGTH - j]) for j in range(1, HALF)] + [None]
    return cos_forward(LENGTH, e), sin_forward(LENGTH, o)


def tables():
    def table(rows, cols):
        angle = (np.outer(np.arange(rows), np.arange(cols)) % WIDE).astype(np.float32)
        angle = angle * np.float32(2.0 * math.pi / WIDE)
        return np.cos(angle), np.sin(angle)

    c, s = table(WIDE, WIDE)
    first = np.block([[c, -s], [s, c]])
    second = np.block([[c, s], [-s, c]])
    small_z, small_y = [], []
    for flip in (False, True):
        c, s = table(EDGE, WIDE)
        if flip:
            c, s = c[::-1], s[::-1]
        small_z.append(np.block([[c, -s], [s, c]]))
        small_y.append(np.block([[c.T, s.T], [-s.T, c.T]]))
    return [
        jnp.asarray(t.astype(np.float32)).astype(BF16)
        for t in (first, second, np.stack(small_z), np.stack(small_y))
    ]


def dot(a, b):
    return jnp.dot(a, b, preferred_element_type=F32)


def spot(k):
    return k // 2, (k % 2) * WIDE


def split(value):
    high = value.astype(BF16)
    rest = value - high.astype(F32)
    middle = rest.astype(BF16)
    return high, middle, (rest - middle.astype(F32)).astype(BF16)


def load_rows(tomo_ref, near_ref, far_ref, at):
    s = []
    for ref, count in ((tomo_ref, SLAB), (near_ref, SLAB), (far_ref, SLAB - 1)):
        s += [ref[j, at, :].astype(F32) for j in range(count)]
    return s


def either(core, one, two, run):
    @pl.when(core == 0)
    def _():
        run(one, two)

    @pl.when(core != 0)
    def _():
        run(two, one)


def factor_kernel(core_ref, tomo_hbm, own_ref, other_ref, factor_ref, tomo_ref, sum_ref, square_ref, tomo_sem):
    fetch = pltpu.make_async_copy(tomo_hbm, tomo_ref, tomo_sem)
    fetch.start()
    volume = float(EDGE**3)
    ahead = lax.broadcasted_iota(jnp.int32, (WIDE, WIDE), 0) - lax.broadcasted_iota(jnp.int32, (WIDE, WIDE), 1)
    band = (jnp.where(ahead < 0, ahead + WIDE, ahead) < EDGE).astype(F32).astype(BF16)
    band = jnp.concatenate([band] * 3, axis=0)
    fetch.wait()

    def along_x(near_ref, far_ref):
        def windows(step, carry):
            at = pl.ds(pl.multiple_of(step * 16, 16), 16)
            s = load_rows(tomo_ref, near_ref, far_ref, at)
            for target, field in ((sum_ref, s), (square_ref, [value * value for value in s])):
                for reach in (1, 2, 4, 8, 16):
                    field = [field[j] + field[j + reach] for j in range(len(field) - reach)]
                for x in range(SLAB):
                    target[x, at, :] = field[x]
            return carry

        lax.fori_loop(0, WIDE // 16, windows, 0)

    either(core_ref[0], own_ref, other_ref, along_x)

    def along_y(field):
        for reach in (1, 2, 4, 8, 16):
            field = field + pltpu.roll(field, WIDE - reach, 0)
        return jnp.concatenate(split(field), axis=1)

    def scale(x, carry):
        both = jnp.concatenate([along_y(sum_ref[x]), along_y(square_ref[x])], axis=0)
        box = dot(both, band) / volume
        mean_t, mean_sq = box[:WIDE], box[WIDE:]
        root = lax.rsqrt(mean_sq - mean_t * mean_t + 1e-05) / jnp.float32(math.sqrt(volume))
        factor_ref[x] = root * jnp.float32(2.0 / (LENGTH * WIDE * WIDE))
        return carry

    lax.fori_loop(0, SLAB, scale, 0, unroll=4)


def spectrum_kernel(core_ref, tomo_ref, own_ref, other_ref, first_ref, second_ref, spec_ref, x_ref, z_ref):
    def along_x(near_ref, far_ref):
        def rows(step, carry):
            at = pl.ds(pl.multiple_of(step * 16, 16), 16)
            real, imag = slices_forward(load_rows(tomo_ref, near_ref, far_ref, at) + [None])
            for k in range(FREQS):
                x_ref[k, at, :WIDE] = real[k].astype(BF16)
                if imag[k] is None:
                    x_ref[k, at, WIDE:] = jnp.zeros((16, WIDE), BF16)
                else:
                    x_ref[k, at, WIDE:] = (-imag[k]).astype(BF16)
            return carry

        lax.fori_loop(0, WIDE // 16, rows, 0)

    either(core_ref[0], own_ref, other_ref, along_x)

    for k in range(FREQS):
        pair, lane = spot(k)
        moved = dot(x_ref[k], first_ref[...]).astype(BF16)
        z_ref[pair, :WIDE, lane:lane + WIDE] = moved[:, :WIDE]
        z_ref[pair, WIDE:, lane:lane + WIDE] = moved[:, WIDE:]
    for pair in range(PAIRS):
        width = WIDE if pair == PAIRS - 1 else 2 * WIDE
        spec_ref[pair, :, :width] = dot(second_ref[...], z_ref[pair, :, :width]).astype(BF16)
        if width == WIDE:
            spec_ref[pair, :, WIDE:] = jnp.zeros((2 * WIDE, WIDE), BF16)


def factor_call(core, tomogram, own, other):
    vmem = pl.BlockSpec(memory_space=pltpu.VMEM)
    return pl.pallas_call(
        factor_kernel,
        out_shape=(
            jax.ShapeDtypeStruct((SLAB, WIDE, WIDE), F32),
            jax.ShapeDtypeStruct((SLAB, WIDE, WIDE), BF16),
        ),
        in_specs=[pl.BlockSpec(memory_space=pltpu.SMEM), pl.BlockSpec(memory_space=pl.ANY), vmem, vmem],
        out_specs=(vmem, vmem),
        scratch_shapes=[
            pltpu.VMEM((SLAB, WIDE, WIDE), F32),
            pltpu.VMEM((SLAB, WIDE, WIDE), F32),
            pltpu.SemaphoreType.DMA,
        ],
        compiler_params=pltpu.CompilerParams(vmem_limit_bytes=8 << 20),
        cost_estimate=pl.CostEstimate(flops=4_000_000_000, transcendentals=0, bytes_accessed=6_000_000),
        name="factor",
    )(core, tomogram, own, other)


def spectrum_call(core, tomogram, own, other, first, second):
    vmem = pl.BlockSpec(memory_space=pltpu.VMEM)
    return pl.pallas_call(
        spectrum_kernel,
        out_shape=jax.ShapeDtypeStruct((PAIRS, 2 * WIDE, 2 * WIDE), BF16),
        in_specs=[pl.BlockSpec(memory_space=pltpu.SMEM)] + [vmem] * 5,
        out_specs=vmem,
        scratch_shapes=[
            pltpu.VMEM((FREQS, WIDE, 2 * WIDE), BF16),
            pltpu.VMEM((PAIRS, 2 * WIDE, 2 * WIDE), BF16),
        ],
        compiler_params=pltpu.CompilerParams(vmem_limit_bytes=10 << 20),
        cost_estimate=pl.CostEstimate(flops=4_000_000_000, transcendentals=0, bytes_accessed=6_000_000),
        name="spectrum",
    )(core, tomogram, own, other, first, second)


def prep_kernel(core_ref, temp_ref, packed_ref):
    values = temp_ref[0].astype(F32).reshape(SLAB * EDGE, EDGE)
    rows = 4 * EDGE
    packed = jnp.concatenate([values[g * rows:(g + 1) * rows] for g in range(4)], axis=1).astype(BF16)
    for member in range(packed_ref.shape[0]):
        packed_ref[member] = packed


def prep_call(core, templates, members):
    return pl.pallas_call(
        prep_kernel,
        out_shape=jax.ShapeDtypeStruct((members, WIDE, WIDE), BF16),
        grid_spec=pltpu.PrefetchScalarGridSpec(
            num_scalar_prefetch=1,
            grid=(1,),
            in_specs=[
                pl.BlockSpec((1, EDGE // 2, EDGE, EDGE), lambda i, core: (0, core[0], 0, 0)),
            ],
            out_specs=pl.BlockSpec((members, WIDE, WIDE), lambda i, core: (0, 0, 0)),
        ),
        name="prep",
    )(core, templates)


def turns_of(index):
    order, flips = lax.div(index, 4), lax.rem(index, 4)
    turn_a = (order == 2) | (order == 3) | (order == 4)
    turn_b = (order == 1) | (order == 2) | (order == 4) | (order == 5)
    turn_c = (order == 1) | (order == 4)
    middle = ((flips == 1) | (flips == 2)).astype(jnp.int32)
    flip_x = jnp.where(order >= 3, 1 - middle, middle)
    return (turn_a, turn_b, turn_c), (flip_x, lax.rem(flips, 2), lax.div(flips, 2))


def swap_last(source, target):
    for a in range(EDGE):
        at = slice(a * EDGE, (a + 1) * EDGE)
        target[at, :] = source[at, :].T


def swap_first(source, target):
    for b in range(EDGE):
        target[b * EDGE:(b + 1) * EDGE, :] = source[pl.ds(b, EDGE, stride=EDGE), :]


def turn(base_ref, cube_ref, spare_ref, turns):
    source = base_ref
    for asked, swap, target in zip(turns, (swap_last, swap_first, swap_last), (cube_ref, spare_ref, cube_ref)):
        def moved(swap=swap, source=source, target=target):
            swap(source, target)

        def kept(source=source, target=target):
            target[...] = source[...]

        pl.when(asked)(moved)
        pl.when(jnp.logical_not(asked))(kept)
        source = target


def match_kernel(core_ref, orient_ref, across_ref, own_ref, other_ref, spec_ref, factor_ref, first_ref, second_ref,
                 small_z_ref, small_y_ref, best_ref,
                 base_ref, cube_ref, spare_ref, packed_ref, a_ref, z_ref, p_ref, q_ref, f_ref):
    core = core_ref[0]
    halves = [ref[...].astype(F32) for ref in (own_ref, other_ref)]
    total = float(EDGE**3)
    center = jnp.sum(halves[0] + halves[1]) / total
    halves = [half - center for half in halves]
    spread = jnp.sum(halves[0] * halves[0] + halves[1] * halves[1]) / total
    root = lax.rsqrt(spread + 1e-05)
    for mine, half in zip((core, 1 - core), halves):
        half = (half * root).astype(BF16).astype(F32)
        for group in range(4):
            start = pl.multiple_of((16 * mine + 4 * group) * EDGE, 128)
            base_ref[pl.ds(start, 4 * EDGE), :] = half[:, group * EDGE:(group + 1) * EDGE]

    flips = []
    for o, index in enumerate((orient_ref[0], across_ref[0])):
        turns, flipped = turns_of(index)
        flips.append(flipped)
        turn(base_ref, cube_ref.at[o], spare_ref.at[o], turns)

    for o in range(2):
        for x in range(EDGE):
            tile = cube_ref[o, x * EDGE:(x + 1) * EDGE, :]
            packed_ref[o, x] = jnp.concatenate([tile[8 * g:8 * g + 8] for g in range(4)], axis=1)

    for o in range(2):
        s = [None] * LENGTH
        for i in range(EDGE):
            s[i + SLAB // 2] = packed_ref[o, jnp.where(flips[o][0] == 1, EDGE - 1 - i, i)]
        real, imag = slices_forward(s)
        for k in range(FREQS):
            share = 0.5 if k in (0, HALF) else 1.0
            for g in range(4):
                at = slice(k * EDGE + 8 * g, k * EDGE + 8 * g + 8)
                lanes = slice(g * EDGE, (g + 1) * EDGE)
                a_ref[o, at, :EDGE] = real[k][:, lanes] * jnp.float32(share)
                if imag[k] is None:
                    a_ref[o, at, EDGE:2 * EDGE] = jnp.zeros((8, EDGE), F32)
                else:
                    a_ref[o, at, EDGE:2 * EDGE] = -imag[k][:, lanes]

    for o in range(2):
        moved = dot(a_ref[o].astype(BF16), small_z_ref[flips[o][2]]).astype(BF16)
        for k in range(FREQS):
            pair, lane = spot(k)
            part = moved[k * EDGE:(k + 1) * EDGE]
            z_ref[o, pair, :EDGE, lane:lane + WIDE] = part[:, :WIDE]
            z_ref[o, pair, EDGE:, lane:lane + WIDE] = part[:, WIDE:]

    for pair in range(PAIRS):
        width = WIDE if pair == PAIRS - 1 else 2 * WIDE
        slab = spec_ref[pair, :, :width].astype(F32)
        slab_r, slab_i = slab[:WIDE], slab[WIDE:]
        for o in range(2):
            temp = dot(small_y_ref[flips[o][1]], z_ref[o, pair, :, :width])
            temp_r, temp_i = temp[:WIDE], temp[WIDE:]
            prod_r = (slab_r * temp_r + slab_i * temp_i).astype(BF16)
            prod_i = (slab_i * temp_r - slab_r * temp_i).astype(BF16)
            for part in range(width // WIDE):
                k = 2 * pair + part
                lanes = slice(part * WIDE, (part + 1) * WIDE)
                p_ref[o, k, :, :WIDE] = prod_r[:, lanes]
                p_ref[o, k, :, WIDE:] = prod_i[:, lanes]

    for o in range(2):
        for k in range(FREQS):
            pair, lane = spot(k)
            moved = dot(p_ref[o, k], second_ref[...]).astype(BF16)
            q_ref[o, pair, :WIDE, lane:lane + WIDE] = moved[:, :WIDE]
            q_ref[o, pair, WIDE:, lane:lane + WIDE] = moved[:, WIDE:]
    for o in range(2):
        for pair in range(PAIRS):
            width = WIDE if pair == PAIRS - 1 else 2 * WIDE
            f_ref[o, pair, :, :width] = dot(first_ref[...], q_ref[o, pair, :, :width])

    def correlation(o, at):
        fr, fi = [], []
        for k in range(FREQS):
            pair, lane = spot(k)
            fr.append(f_ref[o, pair, pl.ds(at, 8), lane:lane + WIDE])
            fi.append(f_ref[o, pair, pl.ds(WIDE + at, 8), lane:lane + WIDE])
        reach = SLAB // 2
        even = cos_inverse(LENGTH, fr, list(range(reach + 1)))
        odd = sin_inverse(LENGTH, fi, list(range(1, reach + 1)))
        values = []
        for lag in range(-reach, SLAB - reach):
            if lag == 0:
                values.append(even[0])
            elif lag > 0:
                values.append(even[lag] - odd[lag])
            else:
                values.append(even[-lag] + odd[-lag])
        return values

    def scores(block, carry):
        at = pl.multiple_of(block * 16, 16)
        rows = []
        for part in (0, 8):
            pair = [correlation(o, at + part) for o in range(2)]
            rows.append([jnp.maximum(one, two) for one, two in zip(*pair)])
        for x in range(SLAB):
            value = jnp.concatenate([rows[0][x], rows[1][x]], axis=0) * factor_ref[x, pl.ds(at, 16), :]
            best_ref[x, pl.ds(at, 16), :] = value.astype(BF16)
        return carry

    lax.fori_loop(0, WIDE // 16, scores, 0)


def match_call(core, orient, across, own, other, spec, factor, first, second, small_z, small_y):
    vmem = pl.BlockSpec(memory_space=pltpu.VMEM)
    smem = pl.BlockSpec(memory_space=pltpu.SMEM)
    cube = EDGE * EDGE
    return pl.pallas_call(
        match_kernel,
        out_shape=jax.ShapeDtypeStruct((SLAB, WIDE, WIDE), BF16),
        in_specs=[smem] * 3 + [vmem] * 8,
        out_specs=vmem,
        scratch_shapes=[
            pltpu.VMEM((cube, EDGE), F32),
            pltpu.VMEM((2, cube, EDGE), F32),
            pltpu.VMEM((2, cube, EDGE), F32),
            pltpu.VMEM((2, EDGE, 8, WIDE), F32),
            pltpu.VMEM((2, FREQS * EDGE, 2 * EDGE), F32),
            pltpu.VMEM((2, PAIRS, 2 * EDGE, 2 * WIDE), BF16),
            pltpu.VMEM((2, FREQS, WIDE, 2 * WIDE), BF16),
            pltpu.VMEM((2, PAIRS, 2 * WIDE, 2 * WIDE), BF16),
            pltpu.VMEM((2, PAIRS, 2 * WIDE, 2 * WIDE), F32),
        ],
        compiler_params=pltpu.CompilerParams(vmem_limit_bytes=24 << 20),
        cost_estimate=pl.CostEstimate(flops=8_000_000_000, transcendentals=0, bytes_accessed=6_000_000),
        name="match",
    )(core, orient, across, own, other, spec, factor, first, second, small_z, small_y)


def swapped(value, axis):
    return lax.ppermute(value, axis, [(0, 1), (1, 0)])


def from_member(value, axis, root):
    sent = jnp.broadcast_to(value[None], (lax.axis_size(axis), *value.shape))
    got = lax.all_to_all(sent, axis, 0, 0, tiled=True)
    return lax.dynamic_index_in_dim(got, root, 0, keepdims=False)


def halo_pairs(tiles):
    return [
        (2 * tile + core, 2 * (tile - 1 - core) + core)
        for tile in range(tiles)
        for core in range(2)
        if tile - 1 - core >= 0
    ]


def shards(tomogram, templates, owners, orient_ids, slice_mask):
    core_arg = lax.axis_index("core").astype(jnp.int32)[None]
    first, second, small_z, small_y = tables()
    columns = lax.axis_size("tile_2")
    depth, plane = lax.axis_size("tile_0"), lax.axis_size("tile_1") * columns
    root_plane, root_z = lax.rem(owners[0], plane), lax.div(owners[0], plane)

    sent = prep_call(core_arg, templates, plane)
    got = lax.all_to_all(sent, ("tile_1", "tile_2"), 0, 0, tiled=True)
    half = lax.dynamic_index_in_dim(got, root_plane, 0, keepdims=False)

    halo = lax.ppermute(tomogram, TILE + ("core",), halo_pairs(depth * plane))
    across = swapped(orient_ids[0], "far")
    other_halo = swapped(halo, "core")

    half = from_member(half, "tile_0", root_z)
    other_half = swapped(half, "core")

    factor, staged = factor_call(core_arg, tomogram, halo, other_halo)
    spec = spectrum_call(core_arg, staged, halo, other_halo, first, second)

    best = match_call(core_arg, orient_ids[0], across, half, other_half, spec, factor, first, second, small_z, small_y)
    best = jnp.maximum(best, swapped(best, "core"))
    return best.astype(F32) * slice_mask.astype(F32)[:, None, None]


def solution(mesh):
    torus = Mesh(
        mesh.devices.reshape(8, 4, 2, 2, 2), ("tile_0", "tile_1", "tile_2", "far", "core")
    )
    in_specs = (P(TILE, None, None), P(TILE, None, None, None), P(), P(None, ("far", "core")), P(TILE))
    out_specs = P(TILE, None, None)
    return jax.shard_map(
        shards, mesh=torus, in_specs=in_specs, out_specs=out_specs, check_vma=False
    )
```

```python
import math

import jax
import jax.numpy as jnp
import numpy as np
from jax import lax
from jax.experimental import pallas as pl
from jax.experimental.pallas import tpu as pltpu
from jax.sharding import Mesh
from jax.sharding import PartitionSpec as P


TILE = ("tile_0", "tile_1", "tile_2")
EDGE = 32
QUARTER = 64
TAIL = 16
SLAB = 16
WIDE = 128
LENGTH = 48
HALF = LENGTH // 2
FREQS = HALF + 1
PAIRS = (FREQS + 1) // 2
BF16 = jnp.bfloat16
F32 = jnp.float32


def plus(a, b):
    if a is None:
        return b
    return a if b is None else a + b


def minus(a, b):
    if b is None:
        return a
    return -b if a is None else a - b


def weighted(terms):
    total = None
    for value, weight in terms:
        if value is None or abs(weight) < 1e-9:
            continue
        if abs(abs(weight) - 1.0) < 1e-9:
            part = value
        else:
            part = value * jnp.float32(abs(weight))
        if weight > 0:
            total = plus(total, part)
        else:
            total = minus(total, part)
    return total


def cosine(j, k, n):
    return math.cos(2.0 * math.pi * ((j * k) % n) / n)


def sine(j, k, n):
    return math.sin(2.0 * math.pi * ((j * k) % n) / n)


def cos_forward(n, e):
    half = n // 2
    if n % 4:
        return [weighted([(e[j], cosine(j, k, n)) for j in range(half + 1)]) for k in range(half + 1)]
    even = cos_forward(half, e[0::2])
    out = [None] * (half + 1)
    for k in range(n // 4 + 1):
        odd = weighted([(e[j], cosine(j, k, n)) for j in range(1, half, 2)])
        out[k] = plus(even[k], odd)
        if k < n // 4:
            out[half - k] = minus(even[k], odd)
    return out


def sin_forward(n, o):
    half = n // 2
    if n % 4:
        return [weighted([(o[j], sine(j, k, n)) for j in range(1, half)]) if k % half else None for k in range(half + 1)]
    even = sin_forward(half, o[0::2])
    out = [None] * (half + 1)
    for k in range(1, n // 4 + 1):
        odd = weighted([(o[j], sine(j, k, n)) for j in range(1, half, 2)])
        out[k] = plus(even[k], odd) if k < n // 4 else odd
        if k < n // 4:
            out[half - k] = minus(odd, even[k])
    return out


def cos_inverse(n, f, wanted):
    half, quarter = n // 2, n // 4
    if n % 4:
        return {x: weighted([(f[k], cosine(k, x, n)) for k in range(half + 1)]) for x in wanted}
    out = {}
    evens = [x // 2 for x in wanted if x % 2 == 0]
    odds = [x for x in wanted if x % 2]
    if odds:
        q = [minus(f[k], f[half - k]) for k in range(quarter)]
        for x in odds:
            out[x] = weighted([(q[k], cosine(k, x, n)) for k in range(quarter)])
    if evens:
        p = [plus(f[k], f[half - k]) for k in range(quarter)] + [f[quarter]]
        for x, value in cos_inverse(half, p, evens).items():
            out[2 * x] = value
    return out


def sin_inverse(n, g, wanted):
    half, quarter = n // 2, n // 4
    if n % 4:
        return {x: weighted([(g[k], sine(k, x, n)) for k in range(1, half)]) for x in wanted}
    out = {}
    evens = [x // 2 for x in wanted if x % 2 == 0]
    odds = [x for x in wanted if x % 2]
    if odds:
        t = [None] + [plus(g[k], g[half - k]) for k in range(1, quarter)] + [g[quarter]]
        for x in odds:
            out[x] = weighted([(t[k], sine(k, x, n)) for k in range(1, quarter + 1)])
    if evens:
        r = [None] + [minus(g[k], g[half - k]) for k in range(1, quarter)] + [None]
        for x, value in sin_inverse(half, r, evens).items():
            out[2 * x] = value
    return out


def slices_forward(s):
    e = [s[0]] + [plus(s[j], s[LENGTH - j]) for j in range(1, HALF)] + [s[HALF]]
    o = [None] + [minus(s[j], s[LENGTH - j]) for j in range(1, HALF)] + [None]
    return cos_forward(LENGTH, e), sin_forward(LENGTH, o)


def tables():
    def table(rows, cols):
        angle = (np.outer(np.arange(rows), np.arange(cols)) % WIDE).astype(np.float32)
        angle = angle * np.float32(2.0 * math.pi / WIDE)
        return np.cos(angle), np.sin(angle)

    c, s = table(WIDE, WIDE)
    first = np.block([[c, -s], [s, c]])
    second = np.block([[c, s], [-s, c]])
    small_z, small_y = [], []
    for flip in (False, True):
        c, s = table(EDGE, WIDE)
        if flip:
            c, s = c[::-1], s[::-1]
        small_z.append(np.block([[c, -s], [s, c]]))
        small_y.append(np.block([[c.T, s.T], [-s.T, c.T]]))
    return [
        jnp.asarray(t.astype(np.float32)).astype(BF16)
        for t in (first, second, np.stack(small_z), np.stack(small_y))
    ]


def dot(a, b):
    return jnp.dot(a, b, preferred_element_type=F32)


def spot(k):
    return k // 2, (k % 2) * WIDE


def split(value):
    high = value.astype(BF16)
    rest = value - high.astype(F32)
    middle = rest.astype(BF16)
    return high, middle, (rest - middle.astype(F32)).astype(BF16)


def load_rows(tomo_ref, near_ref, far_ref, at):
    s = []
    for ref, count in ((tomo_ref, SLAB), (near_ref, SLAB), (far_ref, SLAB - 1)):
        s += [ref[j, at, :].astype(F32) for j in range(count)]
    return s


def either(core, one, two, run):
    @pl.when(core == 0)
    def _():
        run(one, two)

    @pl.when(core != 0)
    def _():
        run(two, one)


def factor_kernel(core_ref, tomo_hbm, own_ref, other_ref, factor_hbm, tomo_ref,
                  factor_ref, sum_ref, square_ref, tomo_sem, out_sems):
    fetch = pltpu.make_async_copy(tomo_hbm, tomo_ref, tomo_sem)
    fetch.start()
    volume = float(EDGE**3)
    ahead = lax.broadcasted_iota(jnp.int32, (WIDE, WIDE), 0) - lax.broadcasted_iota(jnp.int32, (WIDE, WIDE), 1)
    band = (jnp.where(ahead < 0, ahead + WIDE, ahead) < EDGE).astype(F32).astype(BF16)
    band = jnp.concatenate([band] * 3, axis=0)
    fetch.wait()

    def along_x(near_ref, far_ref):
        def windows(step, carry):
            at = pl.ds(pl.multiple_of(step * 16, 16), 16)
            s = load_rows(tomo_ref, near_ref, far_ref, at)
            for target, field in ((sum_ref, s), (square_ref, [value * value for value in s])):
                for reach in (1, 2, 4, 8, 16):
                    field = [field[j] + field[j + reach] for j in range(len(field) - reach)]
                for x in range(SLAB):
                    target[x, at, :] = field[x]
            return carry

        lax.fori_loop(0, WIDE // 16, windows, 0)

    either(core_ref[0], own_ref, other_ref, along_x)

    def along_y(field):
        for reach in (1, 2, 4, 8, 16):
            field = field + pltpu.roll(field, WIDE - reach, 0)
        return jnp.concatenate(split(field), axis=1)

    def scale(x, carry):
        both = jnp.concatenate([along_y(sum_ref[x]), along_y(square_ref[x])], axis=0)
        box = dot(both, band) / volume
        mean_t, mean_sq = box[:WIDE], box[WIDE:]
        root = lax.rsqrt(mean_sq - mean_t * mean_t + 1e-05) / jnp.float32(math.sqrt(volume))
        factor_ref[x] = root * jnp.float32(2.0 / (LENGTH * WIDE * WIDE))
        return carry

    writes = []
    for part in range(SLAB // 4):
        lax.fori_loop(4 * part, 4 * part + 4, scale, 0, unroll=4)
        at = pl.ds(4 * part, 4)
        writes.append(pltpu.make_async_copy(factor_ref.at[at], factor_hbm.at[at], out_sems.at[part]))
        writes[-1].start()
    for write in writes:
        write.wait()


def spectrum_kernel(core_ref, tomo_ref, own_ref, other_ref, first_ref, second_ref, spec_ref, x_ref, z_ref):
    def along_x(near_ref, far_ref):
        def rows(step, carry):
            at = pl.ds(pl.multiple_of(step * 16, 16), 16)
            real, imag = slices_forward(load_rows(tomo_ref, near_ref, far_ref, at) + [None])
            for k in range(FREQS):
                x_ref[k, at, :WIDE] = real[k].astype(BF16)
                if imag[k] is None:
                    x_ref[k, at, WIDE:] = jnp.zeros((16, WIDE), BF16)
                else:
                    x_ref[k, at, WIDE:] = (-imag[k]).astype(BF16)
            return carry

        lax.fori_loop(0, WIDE // 16, rows, 0)

    either(core_ref[0], own_ref, other_ref, along_x)

    for k in range(FREQS):
        pair, lane = spot(k)
        moved = dot(x_ref[k], first_ref[...]).astype(BF16)
        z_ref[pair, :WIDE, lane:lane + WIDE] = moved[:, :WIDE]
        z_ref[pair, WIDE:, lane:lane + WIDE] = moved[:, WIDE:]
    for pair in range(PAIRS):
        width = WIDE if pair == PAIRS - 1 else 2 * WIDE
        spec_ref[pair, :, :width] = dot(second_ref[...], z_ref[pair, :, :width]).astype(BF16)
        if width == WIDE:
            spec_ref[pair, :, WIDE:] = jnp.zeros((2 * WIDE, WIDE), BF16)


def factor_call(core, tomogram, own, other):
    vmem = pl.BlockSpec(memory_space=pltpu.VMEM)
    hbm = pl.BlockSpec(memory_space=pltpu.HBM)
    return pl.pallas_call(
        factor_kernel,
        out_shape=(
            jax.ShapeDtypeStruct((SLAB, WIDE, WIDE), F32),
            jax.ShapeDtypeStruct((SLAB, WIDE, WIDE), BF16),
        ),
        in_specs=[pl.BlockSpec(memory_space=pltpu.SMEM), hbm, vmem, vmem],
        out_specs=(hbm, vmem),
        scratch_shapes=[
            pltpu.VMEM((SLAB, WIDE, WIDE), F32),
            pltpu.VMEM((SLAB, WIDE, WIDE), F32),
            pltpu.VMEM((SLAB, WIDE, WIDE), F32),
            pltpu.SemaphoreType.DMA,
            pltpu.SemaphoreType.DMA((SLAB // 4,)),
        ],
        compiler_params=pltpu.CompilerParams(vmem_limit_bytes=8 << 20),
        cost_estimate=pl.CostEstimate(flops=4_000_000_000, transcendentals=0, bytes_accessed=6_000_000),
        name="factor",
    )(core, tomogram, own, other)


def spectrum_call(core, tomogram, own, other, first, second):
    vmem = pl.BlockSpec(memory_space=pltpu.VMEM)
    return pl.pallas_call(
        spectrum_kernel,
        out_shape=jax.ShapeDtypeStruct((PAIRS, 2 * WIDE, 2 * WIDE), BF16),
        in_specs=[pl.BlockSpec(memory_space=pltpu.SMEM)] + [vmem] * 5,
        out_specs=vmem,
        scratch_shapes=[
            pltpu.VMEM((FREQS, WIDE, 2 * WIDE), BF16),
            pltpu.VMEM((PAIRS, 2 * WIDE, 2 * WIDE), BF16),
        ],
        compiler_params=pltpu.CompilerParams(vmem_limit_bytes=10 << 20),
        cost_estimate=pl.CostEstimate(flops=4_000_000_000, transcendentals=0, bytes_accessed=6_000_000),
        name="spectrum",
    )(core, tomogram, own, other, first, second)


def prep_kernel(core_ref, far_ref, orient_ref, temp_ref, packed_ref):
    values = temp_ref[0].astype(F32).reshape(SLAB * EDGE, EDGE)
    rows = 4 * EDGE
    packed = jnp.concatenate([values[g * rows:(g + 1) * rows] for g in range(4)], axis=1)
    packed = jnp.where(far_ref[0] == 0, packed[:QUARTER], packed[QUARTER:]).astype(BF16)
    index = jnp.full((TAIL, WIDE), orient_ref[0], jnp.int32).astype(F32).astype(BF16)
    for member in range(packed_ref.shape[0]):
        packed_ref[member, :QUARTER] = packed
        packed_ref[member, QUARTER:] = index


def prep_call(core, far, orient, templates, members):
    shape = (members, QUARTER + TAIL, WIDE)
    return pl.pallas_call(
        prep_kernel,
        out_shape=jax.ShapeDtypeStruct(shape, BF16),
        grid_spec=pltpu.PrefetchScalarGridSpec(
            num_scalar_prefetch=3,
            grid=(1,),
            in_specs=[
                pl.BlockSpec((1, EDGE // 2, EDGE, EDGE), lambda i, core, far, orient: (0, core[0], 0, 0)),
            ],
            out_specs=pl.BlockSpec(shape, lambda i, core, far, orient: (0, 0, 0)),
        ),
        name="prep",
    )(core, far, orient, templates)


def turns_of(index):
    order, flips = lax.div(index, 4), lax.rem(index, 4)
    turn_a = (order == 2) | (order == 3) | (order == 4)
    turn_b = (order == 1) | (order == 2) | (order == 4) | (order == 5)
    turn_c = (order == 1) | (order == 4)
    middle = ((flips == 1) | (flips == 2)).astype(jnp.int32)
    flip_x = jnp.where(order >= 3, 1 - middle, middle)
    return (turn_a, turn_b, turn_c), (flip_x, lax.rem(flips, 2), lax.div(flips, 2))


def swap_last(source, target):
    for a in range(EDGE):
        at = slice(a * EDGE, (a + 1) * EDGE)
        target[at, :] = source[at, :].T


def swap_first(source, target):
    for b in range(EDGE):
        target[b * EDGE:(b + 1) * EDGE, :] = source[pl.ds(b, EDGE, stride=EDGE), :]


def turn(base_ref, cube_ref, spare_ref, turns):
    source = base_ref
    for asked, swap, target in zip(turns, (swap_last, swap_first, swap_last), (cube_ref, spare_ref, cube_ref)):
        def moved(swap=swap, source=source, target=target):
            swap(source, target)

        def kept(source=source, target=target):
            target[...] = source[...]

        pl.when(asked)(moved)
        pl.when(jnp.logical_not(asked))(kept)
        source = target


def match_kernel(core_ref, own_ref, other_ref, spec_ref, factor_hbm, first_ref, second_ref,
                 small_z_ref, small_y_ref, best_ref,
                 factor_ref, base_ref, cube_ref, spare_ref, packed_ref, a_ref, z_ref, p_ref, q_ref, f_ref,
                 factor_sem):
    core = core_ref[0]
    fetch = pltpu.make_async_copy(factor_hbm, factor_ref, factor_sem)
    fetch.start()
    halves = [
        jnp.concatenate([ref[0, :QUARTER], ref[1, :QUARTER]], axis=0).astype(F32) for ref in (own_ref, other_ref)
    ]
    orients = [jnp.max(own_ref[o, QUARTER:].astype(F32)).astype(jnp.int32) for o in range(2)]
    total = float(EDGE**3)
    center = jnp.sum(halves[0] + halves[1]) / total
    halves = [half - center for half in halves]
    spread = jnp.sum(halves[0] * halves[0] + halves[1] * halves[1]) / total
    root = lax.rsqrt(spread + 1e-05)
    for mine, half in zip((core, 1 - core), halves):
        half = (half * root).astype(BF16).astype(F32)
        for group in range(4):
            start = pl.multiple_of((16 * mine + 4 * group) * EDGE, 128)
            base_ref[pl.ds(start, 4 * EDGE), :] = half[:, group * EDGE:(group + 1) * EDGE]

    flips = []
    for o, index in enumerate(orients):
        turns, flipped = turns_of(index)
        flips.append(flipped)
        turn(base_ref, cube_ref.at[o], spare_ref.at[o], turns)

    for o in range(2):
        for x in range(EDGE):
            tile = cube_ref[o, x * EDGE:(x + 1) * EDGE, :]
            packed_ref[o, x] = jnp.concatenate([tile[8 * g:8 * g + 8] for g in range(4)], axis=1)

    for o in range(2):
        s = [None] * LENGTH
        for i in range(EDGE):
            s[i + SLAB // 2] = packed_ref[o, jnp.where(flips[o][0] == 1, EDGE - 1 - i, i)]
        real, imag = slices_forward(s)
        for k in range(FREQS):
            share = 0.5 if k in (0, HALF) else 1.0
            for g in range(4):
                at = slice(k * EDGE + 8 * g, k * EDGE + 8 * g + 8)
                lanes = slice(g * EDGE, (g + 1) * EDGE)
                a_ref[o, at, :EDGE] = real[k][:, lanes] * jnp.float32(share)
                if imag[k] is None:
                    a_ref[o, at, EDGE:2 * EDGE] = jnp.zeros((8, EDGE), F32)
                else:
                    a_ref[o, at, EDGE:2 * EDGE] = -imag[k][:, lanes]

    for o in range(2):
        moved = dot(a_ref[o].astype(BF16), small_z_ref[flips[o][2]]).astype(BF16)
        for k in range(FREQS):
            pair, lane = spot(k)
            part = moved[k * EDGE:(k + 1) * EDGE]
            z_ref[o, pair, :EDGE, lane:lane + WIDE] = part[:, :WIDE]
            z_ref[o, pair, EDGE:, lane:lane + WIDE] = part[:, WIDE:]

    for pair in range(PAIRS):
        width = WIDE if pair == PAIRS - 1 else 2 * WIDE
        slab = spec_ref[pair, :, :width].astype(F32)
        slab_r, slab_i = slab[:WIDE], slab[WIDE:]
        for o in range(2):
            temp = dot(small_y_ref[flips[o][1]], z_ref[o, pair, :, :width])
            temp_r, temp_i = temp[:WIDE], temp[WIDE:]
            prod_r = (slab_r * temp_r + slab_i * temp_i).astype(BF16)
            prod_i = (slab_i * temp_r - slab_r * temp_i).astype(BF16)
            for part in range(width // WIDE):
                k = 2 * pair + part
                lanes = slice(part * WIDE, (part + 1) * WIDE)
                p_ref[o, k, :, :WIDE] = prod_r[:, lanes]
                p_ref[o, k, :, WIDE:] = prod_i[:, lanes]

    for o in range(2):
        for k in range(FREQS):
            pair, lane = spot(k)
            moved = dot(p_ref[o, k], second_ref[...]).astype(BF16)
            q_ref[o, pair, :WIDE, lane:lane + WIDE] = moved[:, :WIDE]
            q_ref[o, pair, WIDE:, lane:lane + WIDE] = moved[:, WIDE:]
    for o in range(2):
        for pair in range(PAIRS):
            width = WIDE if pair == PAIRS - 1 else 2 * WIDE
            f_ref[o, pair, :, :width] = dot(first_ref[...], q_ref[o, pair, :, :width])

    def correlation(o, at):
        fr, fi = [], []
        for k in range(FREQS):
            pair, lane = spot(k)
            fr.append(f_ref[o, pair, pl.ds(at, 8), lane:lane + WIDE])
            fi.append(f_ref[o, pair, pl.ds(WIDE + at, 8), lane:lane + WIDE])
        reach = SLAB // 2
        even = cos_inverse(LENGTH, fr, list(range(reach + 1)))
        odd = sin_inverse(LENGTH, fi, list(range(1, reach + 1)))
        values = []
        for lag in range(-reach, SLAB - reach):
            if lag == 0:
                values.append(even[0])
            elif lag > 0:
                values.append(even[lag] - odd[lag])
            else:
                values.append(even[-lag] + odd[-lag])
        return values

    def scores(block, carry):
        at = pl.multiple_of(block * 16, 16)
        rows = []
        for part in (0, 8):
            pair = [correlation(o, at + part) for o in range(2)]
            rows.append([jnp.maximum(one, two) for one, two in zip(*pair)])
        for x in range(SLAB):
            value = jnp.concatenate([rows[0][x], rows[1][x]], axis=0) * factor_ref[x, pl.ds(at, 16), :]
            best_ref[x, pl.ds(at, 16), :] = value.astype(BF16)
        return carry

    fetch.wait()
    lax.fori_loop(0, WIDE // 16, scores, 0)


def match_call(core, own, other, spec, factor, first, second, small_z, small_y):
    vmem = pl.BlockSpec(memory_space=pltpu.VMEM)
    smem = pl.BlockSpec(memory_space=pltpu.SMEM)
    hbm = pl.BlockSpec(memory_space=pltpu.HBM)
    cube = EDGE * EDGE
    return pl.pallas_call(
        match_kernel,
        out_shape=jax.ShapeDtypeStruct((SLAB, WIDE, WIDE), BF16),
        in_specs=[smem, vmem, vmem, vmem, hbm] + [vmem] * 4,
        out_specs=vmem,
        scratch_shapes=[
            pltpu.VMEM((SLAB, WIDE, WIDE), F32),
            pltpu.VMEM((cube, EDGE), F32),
            pltpu.VMEM((2, cube, EDGE), F32),
            pltpu.VMEM((2, cube, EDGE), F32),
            pltpu.VMEM((2, EDGE, 8, WIDE), F32),
            pltpu.VMEM((2, FREQS * EDGE, 2 * EDGE), F32),
            pltpu.VMEM((2, PAIRS, 2 * EDGE, 2 * WIDE), BF16),
            pltpu.VMEM((2, FREQS, WIDE, 2 * WIDE), BF16),
            pltpu.VMEM((2, PAIRS, 2 * WIDE, 2 * WIDE), BF16),
            pltpu.VMEM((2, PAIRS, 2 * WIDE, 2 * WIDE), F32),
            pltpu.SemaphoreType.DMA,
        ],
        compiler_params=pltpu.CompilerParams(vmem_limit_bytes=24 << 20),
        cost_estimate=pl.CostEstimate(flops=8_000_000_000, transcendentals=0, bytes_accessed=6_000_000),
        name="match",
    )(core, own, other, spec, factor, first, second, small_z, small_y)


def swapped(value, axis):
    return lax.ppermute(value, axis, [(0, 1), (1, 0)])


def halo_pairs(tiles):
    return [
        (2 * tile + core, 2 * (tile - 1 - core) + core)
        for tile in range(tiles)
        for core in range(2)
        if tile - 1 - core >= 0
    ]


def shards(tomogram, templates, owners, orient_ids, slice_mask):
    core_arg = lax.axis_index("core").astype(jnp.int32)[None]
    first, second, small_z, small_y = tables()
    far_arg = lax.axis_index("far").astype(jnp.int32)[None]
    depth, plane = lax.axis_size("tile_0"), lax.axis_size(("tile_1", "tile_2"))
    root_plane, root_z = lax.rem(owners[0], plane), lax.div(owners[0], plane)

    sent = prep_call(core_arg, far_arg, orient_ids[0], templates, depth)
    got = lax.all_to_all(sent, "tile_0", 0, 0, tiled=True)
    part = lax.dynamic_index_in_dim(got, root_z, 0, keepdims=False)

    halo = lax.ppermute(tomogram, TILE + ("core",), halo_pairs(depth * plane))
    other_halo = swapped(halo, "core")

    sent = jnp.broadcast_to(part[None], (2 * plane, *part.shape))
    got = lax.all_to_all(sent, ("tile_1", "tile_2", "far"), 0, 0, tiled=True)
    quarters = lax.dynamic_slice_in_dim(got, 2 * root_plane, 2, 0)
    other_quarters = swapped(quarters, "core")

    factor, staged = factor_call(core_arg, tomogram, halo, other_halo)
    spec = spectrum_call(core_arg, staged, halo, other_halo, first, second)

    best = match_call(
        core_arg, quarters, other_quarters, spec, factor, first, second, small_z, small_y
    )
    best = jnp.maximum(best, swapped(best, "core"))
    return best.astype(F32) * slice_mask.astype(F32)[:, None, None]


def solution(mesh):
    torus = Mesh(
        mesh.devices.reshape(8, 4, 2, 2, 2), ("tile_0", "tile_1", "tile_2", "far", "core")
    )
    in_specs = (P(TILE, None, None), P(TILE, None, None, None), P(), P(None, ("far", "core")), P(TILE))
    out_specs = P(TILE, None, None)
    return jax.shard_map(
        shards, mesh=torus, in_specs=in_specs, out_specs=out_specs, check_vma=False
    )
```
